128 devices in a mesh: group: 16 (over y, x_hi, core), tp: 8 (over z, x_lo).
Axes of the slice: x: 4 (x_hi: 2, x_lo: 2; x = x_hi * 2 + x_lo), y: 4, z: 4, core: 2. Of those that a mesh axis runs over, the one named last changes fastest.
Arguments:
- prefix_kv: bfloat16 [8, 16384, 256], P('tp'), may hold values from -4 to 4
- cached_node_states: bfloat16 [8, 480, 64, 256], P('tp', 'group'), may hold values from -4 to 4
- fresh_hidden: bfloat16 [2048, 8192], P(('group', 'tp')), may hold values from -6 to 6
- key_value_weight: bfloat16 [8192, 2048], P(None, 'tp'), may hold values from -0.0625 to 0.0625
- key_value_bias: bfloat16 [2048], P('tp'), may hold values from -3 to 3
- decode_q: bfloat16 [2048, 8192], P('group', 'tp'), may hold values from -128 to 128
- decoded_key_value: bfloat16 [8, 2048, 256], P('tp', 'group'), may hold values from -8 to 8
- parent: int32 [512], replicated, may hold values from -1 to 511, as said below
- child_parent: int32 [16], replicated, may hold values from 0 to 511, as said below
- node_len: int32 [512], replicated, may hold values from 1 to 64
Outputs:
- attended: bfloat16 [2048, 8192], P('group', 'tp')
The draws below stay inside these ranges and needn't reach their ends.
Inputs may be any that keep to these rules, and one draw needn't show every extreme that they name: `parent`: node n is held by group n // 32. Parents lead from any node to a root within 64 nodes. All nodes at one depth are held by one group, and each group's nodes lie at 4 depths, 8 at each, so a path holds at most 4 nodes of one group. `child_parent`: every path from a child's parent holds at most 64 nodes and at most 4 of any group; at least one child's path has exactly 64 nodes, 4 of every group.
All inputs are finite; a program needn't handle non-finite values.
Results may differ from the reference program's by a relative error of at most 0.0038.
Values may be sent and summed in bfloat16 or wider, within the bound.
No kernel may reach another device: no remote copies, remote signals or barrier semaphores. Data moves between devices by JAX's collectives and lax.ppermute only.
A program may use at most 128 MiB of HBM per device.

```python
import jax
import jax.numpy as jnp
from jax import lax

MODEL_WIDTH = 8192
QUERY_HEADS = 64
KEY_VALUE_HEADS = 8
HEAD_SIZE = 128
STEP_SLOTS = 64
PATH_LIMIT = 64
FRESH_NODES = 2
DSTEPS = 4
PROMPT_TOKENS = 16384
NPG = 32
GROUP_ROWS = 128
QUERY_ROW_TOTAL = 2048
TREE_NODES = 512
CACHED_NODES = 30
SLOTS = 4
FROWS = 2048
N_GROUP = 16


def tree_layout(key):
    tree_key = jax.random.fold_in(key, 7)
    random_key_first, random_key_second, random_key_third, key_four, key_five = jax.random.split(tree_key, 5)
    group_count = TREE_NODES // NPG
    branch_width = NPG // SLOTS
    depth_order = jax.random.permutation(random_key_first, group_count).astype(jnp.int32)
    depth_rank = jnp.zeros((group_count,), jnp.int32).at[depth_order].set(jnp.arange(group_count, dtype=jnp.int32))
    node_ids = jnp.arange(TREE_NODES, dtype=jnp.int32)
    owner_group = node_ids // NPG
    inner_index = node_ids % NPG
    path_depth = depth_rank[owner_group] + group_count * (inner_index // branch_width)
    parent_pick = jax.random.randint(random_key_second, (TREE_NODES,), 0, branch_width)
    upper_depth = path_depth - 1
    upper_group = depth_order[upper_depth % group_count]
    upper_node = upper_group * NPG + upper_depth // group_count * branch_width + parent_pick
    parents = jnp.where(path_depth > 0, upper_node, -1).astype(jnp.int32)
    child_nodes = jax.random.randint(random_key_third, (group_count,), 0, TREE_NODES)
    deepest = depth_order[group_count - 1] * NPG + (SLOTS - 1) * branch_width + jax.random.randint(key_four, (), 0, branch_width)
    forced_group = jax.random.randint(key_five, (), 0, group_count)
    child_nodes = jnp.where(jnp.arange(group_count) == forced_group, deepest, child_nodes).astype(jnp.int32)
    return (parents, child_nodes)


def draw_parent(key, part):
    parents, child_nodes = tree_layout(key)
    return parents


def draw_child_parent(key, part):
    parents, child_nodes = tree_layout(key)
    return child_nodes


def draw_prefix_kv(key, part):
    self_key_rows = jax.random.fold_in(key, 3)
    sampled_items = jnp.clip(jax.random.normal(self_key_rows, (KEY_VALUE_HEADS, PROMPT_TOKENS, 2 * HEAD_SIZE), dtype=jnp.float32), -4.0, 4.0)
    return sampled_items.astype(jnp.bfloat16)


def draw_decode_q(key, part):
    self_key_rows = jax.random.fold_in(key, 5)
    random_key_first = jax.random.fold_in(self_key_rows, 0)
    sampled_items = jnp.clip(3.0 * jax.random.normal(random_key_first, (QUERY_ROW_TOTAL, QUERY_HEADS * HEAD_SIZE), dtype=jnp.float32), -12.0, 12.0)
    return sampled_items.astype(jnp.bfloat16)


def touch_ends(values, key, least, top_value):
    longest = values.shape.index(max(values.shape))
    spots = []
    for shift in (0, 1):
        where = [jax.random.randint(jax.random.fold_in(key, axis), (), 0, length) for axis, length in enumerate(values.shape)]
        where[longest] = (where[longest] + shift) % values.shape[longest]
        spots.append(tuple(where))
    return values.at[spots[0]].set(least).at[spots[1]].set(top_value)


def level_of(stream_key, shape, shards, smallest, top_value):
    loudness, own = 1.0, jax.random.fold_in(stream_key, 6)
    for position, blocks in shards:
        steps = jnp.exp(jax.random.uniform(jax.random.fold_in(own, position), (blocks,), jnp.float32, smallest / len(shards), top_value / len(shards)))
        loudness = loudness * jnp.repeat(steps, shape[position] // blocks).reshape([-1 if axis == position else 1 for axis in range(len(shape))])
    return loudness


def normal_values(stream_key, dims, scale, limit, cuts=(), kind=jnp.bfloat16):
    drawn = scale * jax.random.normal(stream_key, dims, jnp.float32)
    if cuts:
        drawn = drawn * level_of(stream_key, dims, cuts, -0.22, 0.18)
    return jnp.clip(drawn, -limit, limit).astype(kind)


def setup_inputs(seed: int = 0) -> dict:
    key_list = jax.random.split(jax.random.key(seed), 11)
    prefix_kv = draw_prefix_kv(jax.random.fold_in(key_list[10], 71), 0)
    cached_node_states = normal_values(key_list[1], (KEY_VALUE_HEADS, N_GROUP * CACHED_NODES, STEP_SLOTS, 2 * HEAD_SIZE), 1.0, 4.0, ((0, 8), (1, 16)))
    fresh_hidden = normal_values(key_list[2], (FROWS, MODEL_WIDTH), 1.0, 6.0, ((0, 128),))
    key_value_weight = normal_values(key_list[3], (MODEL_WIDTH, KEY_VALUE_HEADS * 2 * HEAD_SIZE), MODEL_WIDTH ** -0.5, 0.0625, ((1, 8),))
    key_value_bias = normal_values(key_list[4], (KEY_VALUE_HEADS * 2 * HEAD_SIZE,), 0.5, 3.0, ((0, 8),))
    decode_q = draw_decode_q(jax.random.fold_in(key_list[10], 71), 0)
    decoded_key_value = normal_values(key_list[6], (KEY_VALUE_HEADS, QUERY_ROW_TOTAL, 2 * HEAD_SIZE), 2.0, 8.0, ((0, 8), (1, 16)))
    parent = draw_parent(jax.random.fold_in(key_list[10], 71), 0)
    child_parent = draw_child_parent(jax.random.fold_in(key_list[10], 71), 0)
    node_len = touch_ends(jax.random.randint(key_list[9], (TREE_NODES,), 1, STEP_SLOTS + 1), jax.random.fold_in(key_list[9], 1), 1, STEP_SLOTS).astype(jnp.int32)
    return dict(prefix_kv=prefix_kv, cached_node_states=cached_node_states, fresh_hidden=fresh_hidden, key_value_weight=key_value_weight, key_value_bias=key_value_bias, decode_q=decode_q, decoded_key_value=decoded_key_value, parent=parent, child_parent=child_parent, node_len=node_len)


def reference(prefix_kv, cached_node_states, fresh_hidden, key_value_weight, key_value_bias, decode_q, decoded_key_value, parent, child_parent, node_len):
    head_size = HEAD_SIZE
    paired_width = 2 * HEAD_SIZE
    group_share = QUERY_HEADS // KEY_VALUE_HEADS
    query_row_block = group_share * GROUP_ROWS
    projected = jnp.dot(fresh_hidden.astype(jnp.float32), key_value_weight.astype(jnp.float32), preferred_element_type=jnp.float32)
    fresh_key_value = (projected + key_value_bias.astype(jnp.float32)).astype(jnp.bfloat16)
    fresh_key_value = fresh_key_value.reshape(N_GROUP, FRESH_NODES, STEP_SLOTS, KEY_VALUE_HEADS, paired_width).transpose(3, 0, 1, 2, 4)
    earlier_nodes = cached_node_states.reshape(KEY_VALUE_HEADS, N_GROUP, CACHED_NODES, STEP_SLOTS, paired_width)
    node_lookup_table = jnp.concatenate([earlier_nodes, fresh_key_value], axis=2).reshape(KEY_VALUE_HEADS, TREE_NODES, STEP_SLOTS, paired_width)
    row_ids = jnp.arange(GROUP_ROWS)
    own_mask = ((row_ids[:, None] // DSTEPS) == (row_ids[None, :] // DSTEPS)) & ((row_ids[None, :] % DSTEPS) <= (row_ids[:, None] % DSTEPS))
    own_mask = jnp.tile(own_mask, (group_share, 1))

    def one_group(group_id):
        def climb_up(current, unused):
            following = jnp.where(current >= 0, parent[jnp.maximum(current, 0)], -1)
            return following, current

        unused_end, path_nodes = lax.scan(climb_up, child_parent[group_id], None, length=PATH_LIMIT)
        clamped_nodes = jnp.maximum(path_nodes, 0)
        node_lens = jnp.where(path_nodes >= 0, node_len[clamped_nodes], 0)
        path_mask = (jnp.arange(STEP_SLOTS)[None, :] < node_lens[:, None]).reshape(-1)
        path_key_value = node_lookup_table[:, clamped_nodes].reshape(KEY_VALUE_HEADS, PATH_LIMIT * STEP_SLOTS, paired_width)
        row_start = (group_id * GROUP_ROWS).astype(jnp.int32)
        query_matrix = lax.dynamic_slice_in_dim(decode_q, row_start, GROUP_ROWS, 0)
        query_matrix = query_matrix.reshape(GROUP_ROWS, KEY_VALUE_HEADS, group_share, head_size).transpose(1, 2, 0, 3).reshape(KEY_VALUE_HEADS, query_row_block, head_size)
        own_kv = lax.dynamic_slice_in_dim(decoded_key_value, row_start, GROUP_ROWS, 1)
        full_mask = jnp.concatenate([
            jnp.ones((query_row_block, PROMPT_TOKENS), dtype=bool),
            jnp.broadcast_to(path_mask[None, :], (query_row_block, PATH_LIMIT * STEP_SLOTS)),
            own_mask], axis=1)

        def one_head(operands):
            query_head, prefix_head, path_head, own_head = operands
            key_rows = jnp.concatenate([prefix_head, path_head, own_head], axis=0).astype(jnp.float32)
            scores = jnp.dot(query_head.astype(jnp.float32), key_rows[:, :head_size].T, preferred_element_type=jnp.float32) * (head_size ** -0.5)
            scores = jnp.where(full_mask, scores, -1e30)
            row_max = jnp.max(scores, axis=1, keepdims=True)
            weights = jnp.where(full_mask, jnp.exp(scores - row_max), 0.0)
            rounded = lax.optimization_barrier(weights.astype(jnp.bfloat16)).astype(jnp.float32)
            numerator = jnp.dot(rounded, key_rows[:, head_size:], preferred_element_type=jnp.float32)
            return numerator / jnp.sum(weights, axis=1, keepdims=True)

        output_values = lax.map(one_head, (query_matrix, prefix_kv, path_key_value, own_kv))
        output_values = output_values.reshape(KEY_VALUE_HEADS, group_share, GROUP_ROWS, head_size).transpose(2, 0, 1, 3)
        return output_values.reshape(GROUP_ROWS, QUERY_HEADS * HEAD_SIZE).astype(jnp.bfloat16)

    every_group = lax.map(one_group, jnp.arange(N_GROUP, dtype=jnp.int32))
    return every_group.reshape(QUERY_ROW_TOTAL, QUERY_HEADS * HEAD_SIZE)
```

```python
import functools

import jax
import jax.numpy as jnp
from jax import lax
from jax.experimental import pallas as pl
from jax.experimental.pallas import tpu as pltpu
from jax.sharding import PartitionSpec as P

SLOTS = 4
FRESH = 2
SUB = 512
ROWS = 256
BLOCK = 4096
FIRST_BLOCKS = 2
LOW = -1e30
LOG2E = 1.4426950408889634
VMEM_LIMIT = 48 * 2**20


def spec(shape):
    return pl.BlockSpec(shape, lambda *_: (0,) * len(shape))


def lookup(parts, positions):
    low, high = positions & 127, positions >> 7
    result = jnp.zeros_like(positions)
    for row, part in enumerate(parts):
        table = jnp.broadcast_to(part, positions.shape)
        result = jnp.where(high == row, jnp.take_along_axis(table, low, axis=1), result)
    return result


def rows_of(table):
    return [table[row : row + 1, :] for row in range(table.shape[0])]


def ranks(flags):
    width = flags.shape[1]
    before = lax.broadcasted_iota(jnp.int32, (width, width), 0) < lax.broadcasted_iota(
        jnp.int32, (width, width), 1
    )
    return jnp.dot(
        flags.astype(jnp.bfloat16), before.astype(jnp.bfloat16), preferred_element_type=jnp.float32
    )


def slot_sums(held, values, inner, cached_nodes):
    cached = held & (inner < cached_nodes)
    fresh = held & (inner >= cached_nodes)
    rank_cached = ranks(jnp.where(cached, 1.0, 0.0))
    rank_fresh = (SLOTS - 1) - ranks(jnp.where(fresh, 1.0, 0.0))
    slot = jnp.where(cached, rank_cached, rank_fresh)
    return [
        jnp.sum(jnp.where(held & (slot == float(s)), values, 0.0), axis=1, keepdims=True)
        for s in range(SLOTS)
    ]


def route_kernel(groups, parent_ref, child_ref, len_ref, cached_ref, pick_ref, bias_a_ref, bias_b_ref, send_ref, pick_v, pick_s, sem):
    me = lax.axis_index("group")
    cached_nodes = cached_ref.shape[0]
    per_node = cached_nodes + FRESH
    width = 128
    parent = parent_ref[...]
    none = parent.shape[0] * 128
    jump = jnp.where(parent < 0, none, parent)
    lane = lax.broadcasted_iota(jnp.int32, (groups, width), 1)
    path = jnp.where(lane == 0, child_ref[...], none)
    reach = 1
    while reach < 64:
        tables = rows_of(jump)
        ahead = jnp.where(path < none, lookup(tables, jnp.minimum(path, none - 1)), none)
        path = jnp.where((lane >= reach) & (lane < 2 * reach), pltpu.roll(ahead, reach, 1), path)
        jump = jnp.where(jump < none, lookup(tables, jnp.minimum(jump, none - 1)), none)
        reach *= 2
    inner = path % per_node
    there = path < none
    picks = slot_sums(
        there & (path // per_node == me), inner.astype(jnp.float32), inner, cached_nodes
    )
    pick = jnp.zeros((groups, width), jnp.float32)
    for s in range(SLOTS):
        pick = jnp.where(lane == s, picks[s], pick)
    pick = pick.astype(jnp.int32)
    pick_v[...] = pick
    pick_ref[...] = pick
    copy = pltpu.make_async_copy(pick_v, pick_s, sem)
    copy.start()
    group_row = lax.broadcasted_iota(jnp.int32, (groups, width), 0)
    mine = jnp.sum(jnp.where(group_row == me, path, 0).astype(jnp.float32), axis=0, keepdims=True)
    mine = jnp.broadcast_to(mine, (groups, width)).astype(jnp.int32)
    there = mine < none
    lengths = lookup(rows_of(len_ref[...]), jnp.minimum(mine, none - 1)).astype(jnp.float32)
    valid = slot_sums(
        there & (mine // per_node == group_row), lengths, mine % per_node, cached_nodes
    )
    half = width // 2
    token = (lane % half).astype(jnp.float32)
    for ref, first in ((bias_a_ref, 0), (bias_b_ref, 2)):
        limit = jnp.where(lane < half, valid[first], valid[first + 1])
        ref[...] = jnp.where(token < limit, 0.0, LOW)
    copy.wait()
    for g in range(groups):
        for s in range(2):
            node = jnp.minimum(pick_s[g, s], cached_nodes - 1)
            send_ref[g, s] = cached_ref[node]


def route(parent, child_parent, node_len, cached):
    groups = child_parent.shape[0]
    nodes, tokens, width = cached.shape
    rows = parent.shape[0] // 128
    table = jax.ShapeDtypeStruct((groups, 128), jnp.int32)
    bias = jax.ShapeDtypeStruct((groups, 128), jnp.float32)
    out = (table, bias, bias, jax.ShapeDtypeStruct((groups, 2, tokens, width), cached.dtype))
    args = (
        parent.reshape(rows, 128),
        jnp.broadcast_to(child_parent[:, None], (groups, 128)),
        node_len.reshape(rows, 128),
        cached,
    )
    return pl.pallas_call(
        functools.partial(route_kernel, groups),
        out_shape=out,
        in_specs=[spec(a.shape) for a in args],
        out_specs=[spec(o.shape) for o in out],
        scratch_shapes=[
            pltpu.VMEM((groups, 128), jnp.int32),
            pltpu.SMEM((groups, 128), jnp.int32),
            pltpu.SemaphoreType.DMA,
        ],
        name="route",
    )(*args)


def fresh_kernel(pick_ref, hidden_ref, weight_ref, bias_ref, cached_ref, send_ref, total, table):
    step = pl.program_id(0)
    cached_nodes, tokens, width = cached_ref.shape

    @pl.when(step == 0)
    def _():
        total[...] = jnp.zeros_like(total)
        table[:cached_nodes] = cached_ref[...]

    total[...] += jnp.dot(hidden_ref[...], weight_ref[...], preferred_element_type=jnp.float32)

    @pl.when(step == pl.num_programs(0) - 1)
    def _():
        rows = (total[...] + bias_ref[...].astype(jnp.float32)).astype(jnp.bfloat16)
        for f in range(FRESH):
            table[cached_nodes + f] = rows[f * tokens : (f + 1) * tokens]
        for g in range(send_ref.shape[0]):
            for s in range(2):
                node = jnp.clip(pick_ref[g, 2 + s], 0, cached_nodes + FRESH - 1)
                send_ref[g, s] = table[node]


def project_fresh(pick, hidden, weight, bias, cached):
    groups = pick.shape[0]
    nodes, tokens, width = cached.shape
    rows, depth = hidden.shape
    step = 2048
    return pl.pallas_call(
        fresh_kernel,
        grid=(depth // step,),
        out_shape=jax.ShapeDtypeStruct((groups, 2, tokens, width), cached.dtype),
        in_specs=[
            pl.BlockSpec(memory_space=pltpu.SMEM),
            pl.BlockSpec((rows, step), lambda i: (0, i)),
            pl.BlockSpec((step, width), lambda i: (i, 0)),
            spec((1, width)),
            spec(cached.shape),
        ],
        out_specs=spec((groups, 2, tokens, width)),
        scratch_shapes=[
            pltpu.VMEM((rows, width), jnp.float32),
            pltpu.VMEM((nodes + FRESH, tokens, width), cached.dtype),
        ],
        cost_estimate=pl.CostEstimate(
            flops=2 * rows * depth * width, bytes_accessed=8 * 2**20, transcendentals=0
        ),
        name="fresh",
    )(pick, hidden, weight, bias.reshape(1, width), cached)


def take_keys(query, maximum, total, pieces, scale):
    rows = query.shape[0]
    head = query.shape[1]

    def score(c, piece):
        kv, adjust = piece
        s = lax.dot_general(
            query[c * ROWS : (c + 1) * ROWS, :],
            kv[:, :head],
            (((1,), (1,)), ((), ())),
            preferred_element_type=jnp.float32,
        )
        return s if adjust is None else adjust(s)

    def peak(s):
        top = s[:, :128]
        for k in range(1, s.shape[1] // 128):
            top = jnp.maximum(top, s[:, k * 128 : (k + 1) * 128])
        return top

    chunks = rows // ROWS
    now = [score(0, piece) for piece in pieces]
    for c in range(chunks):
        at = slice(c * ROWS, (c + 1) * ROWS)
        top = peak(now[0])
        for s in now[1:]:
            top = jnp.maximum(top, peak(s))
        old = maximum[at, :]
        new = jnp.maximum(old, jnp.max(top, axis=1, keepdims=True) * scale)
        maximum[at, :] = new
        factor = jnp.exp2(old - new)
        acc = total[at, :] * jnp.concatenate([factor, factor], axis=1)
        later = []
        for piece, s in zip(pieces, now):
            if c + 1 < chunks:
                later.append(score(c + 1, piece))
            weights = jnp.exp2(s * scale - new[:, :1]).astype(jnp.bfloat16)
            kv = piece[0]
            values = jnp.concatenate(
                [kv[:, head:], jnp.ones((kv.shape[0], head), jnp.bfloat16)], axis=1
            )
            acc = acc + jnp.dot(weights, values, preferred_element_type=jnp.float32)
        total[at, :] = acc
        now = later


def plain_pieces(ref):
    return [(ref.at[pl.ds(k, SUB), :], None) for k in range(0, ref.shape[0], SUB)]


def masked_pieces(ref, bias_ref):
    def adjust(k, s):
        bias = [bias_ref[row : row + 1, :] for row in range(k // 128, (k + SUB) // 128)]
        return s + jnp.concatenate(bias, axis=1)

    return [
        (ref.at[pl.ds(k, SUB), :], functools.partial(adjust, k))
        for k in range(0, ref.shape[0], SUB)
    ]


def own_piece(ref, steps):
    count = ref.shape[0]

    def adjust(s):
        row = lax.broadcasted_iota(jnp.int32, s.shape, 0) % count
        key = lax.broadcasted_iota(jnp.int32, s.shape, 1)
        seen = (row // steps == key // steps) & (key <= row)
        return jnp.where(seen, s, LOW)

    return [(ref.at[pl.ds(0, count), :], adjust)]


def load_query(q_ref, query):
    rows, head = q_ref.shape[0], query.shape[1]
    for j in range(q_ref.shape[1] // head):
        query[j * rows : (j + 1) * rows, :] = q_ref[:, j * head : (j + 1) * head]


def first_kernel(scale, q_ref, prefix_ref, max_ref, total_ref, query):
    @pl.when(pl.program_id(0) == 0)
    def _():
        load_query(q_ref, query)
        max_ref[...] = jnp.full_like(max_ref, LOW)
        total_ref[...] = jnp.zeros_like(total_ref)

    take_keys(query, max_ref, total_ref, plain_pieces(prefix_ref), scale)


def middle_kernel(scale, steps, blocks, q_ref, prefix_ref, path_ref, bias_ref, own_ref, max_in, total_in, max_ref, total_ref, query):
    step = pl.program_id(0)

    @pl.when(step == 0)
    def _():
        load_query(q_ref, query)
        max_ref[...] = max_in[...]
        total_ref[...] = total_in[...]

    @pl.when(step < blocks)
    def _():
        take_keys(query, max_ref, total_ref, plain_pieces(prefix_ref), scale)

    @pl.when(step == blocks)
    def _():
        pieces = masked_pieces(path_ref, bias_ref) + own_piece(own_ref, steps)
        take_keys(query, max_ref, total_ref, pieces, scale)


def last_kernel(scale, q_ref, path_ref, bias_ref, max_in, total_in, out_ref, query, maximum, total):
    load_query(q_ref, query)
    maximum[...] = max_in[...]
    total[...] = total_in[...]
    take_keys(query, maximum, total, masked_pieces(path_ref, bias_ref), scale)
    rows, head = q_ref.shape[0], query.shape[1]
    for j in range(q_ref.shape[1] // head):
        at = slice(j * rows, (j + 1) * rows)
        out_ref[:, j * head : (j + 1) * head] = (total[at, :head] / total[at, head:]).astype(
            out_ref.dtype
        )


def attention_cost(rows, head, keys):
    return pl.CostEstimate(
        flops=8 * rows * head * keys,
        bytes_accessed=4 * keys * head,
        transcendentals=rows * keys,
    )


def per_device(
    prefix_kv,
    cached_node_states,
    fresh_hidden,
    key_value_weight,
    key_value_bias,
    decode_q,
    decoded_key_value,
    parent,
    child_parent,
    node_len,
):
    steps = 4
    head = prefix_kv.shape[2] // 2
    scale = head ** (-0.5) * LOG2E
    prefix, cached, own = prefix_kv[0], cached_node_states[0], decoded_key_value[0]
    rows = decode_q.shape[0]
    queries = rows * (decode_q.shape[1] // head)
    tp = lax.axis_size("tp")

    hidden = lax.all_to_all(
        jnp.broadcast_to(fresh_hidden[None], (tp,) + fresh_hidden.shape), "tp", 0, 0, tiled=True
    ).reshape(tp * fresh_hidden.shape[0], fresh_hidden.shape[1])
    pick, bias_a, bias_b, send_a = route(parent, child_parent, node_len, cached)
    path_a = lax.all_to_all(send_a, "group", 0, 0, tiled=True).reshape(-1, 2 * head)

    state = (
        jax.ShapeDtypeStruct((queries, 128), jnp.float32),
        jax.ShapeDtypeStruct((queries, 2 * head), jnp.float32),
    )
    params = pltpu.CompilerParams(vmem_limit_bytes=VMEM_LIMIT)
    query_scratch = pltpu.VMEM((queries, head), jnp.bfloat16)
    all_blocks = prefix.shape[0] // BLOCK
    blocks = all_blocks - FIRST_BLOCKS
    maximum, total = pl.pallas_call(
        functools.partial(first_kernel, scale),
        grid=(FIRST_BLOCKS,),
        out_shape=state,
        in_specs=[spec(decode_q.shape), pl.BlockSpec((BLOCK, 2 * head), lambda i: (i, 0))],
        out_specs=[spec(s.shape) for s in state],
        scratch_shapes=[query_scratch],
        compiler_params=params,
        cost_estimate=attention_cost(queries, head, FIRST_BLOCKS * BLOCK),
        name="attend_first",
    )(decode_q, prefix)

    send_b = project_fresh(pick, hidden, key_value_weight, key_value_bias, cached)
    path_b = lax.all_to_all(send_b, "group", 0, 0, tiled=True).reshape(-1, 2 * head)

    maximum, total = pl.pallas_call(
        functools.partial(middle_kernel, scale, steps, blocks),
        grid=(blocks + 1,),
        out_shape=state,
        in_specs=[
            spec(decode_q.shape),
            pl.BlockSpec(
                (BLOCK, 2 * head), lambda i: (jnp.minimum(i + FIRST_BLOCKS, all_blocks - 1), 0)
            ),
            spec(path_a.shape),
            spec(bias_a.shape),
            spec(own.shape),
            spec(state[0].shape),
            spec(state[1].shape),
        ],
        out_specs=[spec(s.shape) for s in state],
        scratch_shapes=[query_scratch],
        compiler_params=params,
        cost_estimate=attention_cost(queries, head, blocks * BLOCK + path_a.shape[0]),
        name="attend_middle",
    )(decode_q, prefix, path_a, bias_a, own, maximum, total)

    return pl.pallas_call(
        functools.partial(last_kernel, scale),
        out_shape=jax.ShapeDtypeStruct(decode_q.shape, jnp.bfloat16),
        in_specs=[spec(a.shape) for a in (decode_q, path_b, bias_b) + state],
        out_specs=spec(decode_q.shape),
        scratch_shapes=[
            query_scratch,
            pltpu.VMEM(state[0].shape, jnp.float32),
            pltpu.VMEM(state[1].shape, jnp.float32),
        ],
        compiler_params=params,
        cost_estimate=attention_cost(queries, head, path_b.shape[0]),
        name="attend_last",
    )(decode_q, path_b, bias_b, maximum, total)


def solution(mesh):
    placed = (
        P("tp", None, None),
        P("tp", "group", None, None),
        P(("group", "tp"), None),
        P(None, "tp"),
        P("tp"),
        P("group", "tp"),
        P("tp", "group", None),
        P(),
        P(),
        P(),
    )
    return jax.shard_map(
        per_device, mesh=mesh, in_specs=placed, out_specs=P("group", "tp"), check_vma=False
    )
```

```python
import functools

import jax
import jax.numpy as jnp
from jax import lax
from jax.experimental import pallas as pl
from jax.experimental.pallas import tpu as pltpu
from jax.sharding import PartitionSpec as P

SLOTS = 4
FRESH = 2
SUB = 512
ROWS = 256
BLOCK = 4096
FIRST_BLOCKS = 2
LOW = -1e30
LOG2E = 1.4426950408889634
VMEM_LIMIT = 56 * 2**20
SMALL_LIMIT = 16 * 2**20


def spec(shape):
    return pl.BlockSpec(shape, lambda *_: (0,) * len(shape))


def lookup(parts, positions):
    low, high = positions & 127, positions >> 7
    result = jnp.zeros_like(positions)
    for row, part in enumerate(parts):
        table = jnp.broadcast_to(part, positions.shape)
        result = jnp.where(high == row, jnp.take_along_axis(table, low, axis=1), result)
    return result


def rows_of(table):
    return [table[row : row + 1, :] for row in range(table.shape[0])]


def ranks(flags):
    width = flags.shape[1]
    before = lax.broadcasted_iota(jnp.int32, (width, width), 0) < lax.broadcasted_iota(
        jnp.int32, (width, width), 1
    )
    return jnp.dot(
        flags.astype(jnp.bfloat16), before.astype(jnp.bfloat16), preferred_element_type=jnp.float32
    )


def slot_sums(held, values, inner, cached_nodes):
    cached = held & (inner < cached_nodes)
    fresh = held & (inner >= cached_nodes)
    rank_cached = ranks(jnp.where(cached, 1.0, 0.0))
    rank_fresh = (SLOTS - 1) - ranks(jnp.where(fresh, 1.0, 0.0))
    slot = jnp.where(cached, rank_cached, rank_fresh)
    return [
        jnp.sum(jnp.where(held & (slot == float(s)), values, 0.0), axis=1, keepdims=True)
        for s in range(SLOTS)
    ]


def route_kernel(groups, parent_ref, child_ref, len_ref, cached_ref, pick_ref, bias_a_ref, bias_b_ref, send_ref, pick_v, pick_s, sem):
    me = lax.axis_index("group")
    cached_nodes = cached_ref.shape[0]
    per_node = cached_nodes + FRESH
    width = 128
    parent = parent_ref[...]
    none = parent.shape[0] * 128
    jump = jnp.where(parent < 0, none, parent)
    lane = lax.broadcasted_iota(jnp.int32, (groups, width), 1)
    group_row = lax.broadcasted_iota(jnp.int32, (groups, width), 0)
    path = jnp.full((groups, width), none, jnp.int32)
    for g in range(groups):
        path = jnp.where((lane == 0) & (group_row == g), child_ref[g], path)
    reach = 1
    while reach < 64:
        tables = rows_of(jump)
        ahead = jnp.where(path < none, lookup(tables, jnp.minimum(path, none - 1)), none)
        path = jnp.where((lane >= reach) & (lane < 2 * reach), pltpu.roll(ahead, reach, 1), path)
        jump = jnp.where(jump < none, lookup(tables, jnp.minimum(jump, none - 1)), none)
        reach *= 2
    inner = path % per_node
    there = path < none
    picks = slot_sums(
        there & (path // per_node == me), inner.astype(jnp.float32), inner, cached_nodes
    )
    pick = jnp.zeros((groups, width), jnp.float32)
    for s in range(SLOTS):
        pick = jnp.where(lane == s, picks[s], pick)
    pick = pick.astype(jnp.int32)
    pick_v[...] = pick
    pick_ref[...] = pick
    copy = pltpu.make_async_copy(pick_v, pick_s, sem)
    copy.start()
    mine = jnp.sum(jnp.where(group_row == me, path, 0).astype(jnp.float32), axis=0, keepdims=True)
    mine = jnp.broadcast_to(mine, (groups, width)).astype(jnp.int32)
    there = mine < none
    lengths = lookup(rows_of(len_ref[...]), jnp.minimum(mine, none - 1)).astype(jnp.float32)
    valid = slot_sums(
        there & (mine // per_node == group_row), lengths, mine % per_node, cached_nodes
    )
    half = width // 2
    token = (lane % half).astype(jnp.float32)
    for ref, first in ((bias_a_ref, 0), (bias_b_ref, 2)):
        limit = jnp.where(lane < half, valid[first], valid[first + 1])
        ref[...] = jnp.where(token < limit, 0.0, LOW)
    copy.wait()
    for g in range(groups):
        for s in range(2):
            node = jnp.minimum(pick_s[g, s], cached_nodes - 1)
            send_ref[g, s] = cached_ref[node]


def route(parent, child_parent, node_len, cached):
    groups = child_parent.shape[0]
    _, tokens, width = cached.shape
    rows = parent.shape[0] // 128
    table = jax.ShapeDtypeStruct((groups, 128), jnp.int32)
    bias = jax.ShapeDtypeStruct((groups, 128), jnp.float32)
    out = (table, bias, bias, jax.ShapeDtypeStruct((groups, 2, tokens, width), cached.dtype))
    args = (
        parent.reshape(rows, 128),
        child_parent,
        node_len.reshape(rows, 128),
        cached,
    )
    return pl.pallas_call(
        functools.partial(route_kernel, groups),
        out_shape=out,
        in_specs=[
            spec(args[0].shape),
            pl.BlockSpec(memory_space=pltpu.SMEM),
            spec(args[2].shape),
            spec(args[3].shape),
        ],
        out_specs=[spec(o.shape) for o in out],
        scratch_shapes=[
            pltpu.VMEM((groups, 128), jnp.int32),
            pltpu.SMEM((groups, 128), jnp.int32),
            pltpu.SemaphoreType.DMA,
        ],
        compiler_params=pltpu.CompilerParams(vmem_limit_bytes=SMALL_LIMIT),
        cost_estimate=pl.CostEstimate(flops=2**24, bytes_accessed=2**21, transcendentals=0),
        name="route",
    )(*args)


def fresh_kernel(parts, pick_ref, *refs):
    hidden_refs = refs[:parts]
    weight_ref, bias_ref, cached_ref, send_ref, total, table, hidden = refs[parts:]
    step = pl.program_id(0)
    me = lax.axis_index("tp")
    cached_nodes, tokens, _ = cached_ref.shape

    @pl.when(step == 0)
    def _():
        total[...] = jnp.zeros_like(total)
        table[:cached_nodes] = cached_ref[...]

    for k, ref in enumerate(hidden_refs):
        block = ref.shape[0]
        hidden[pl.ds(pl.multiple_of((me ^ k) * block, block), block), :] = ref[...]
    total[...] += jnp.dot(hidden[...], weight_ref[...], preferred_element_type=jnp.float32)

    @pl.when(step == pl.num_programs(0) - 1)
    def _():
        rows = (total[...] + bias_ref[...].astype(jnp.float32)[None, :]).astype(jnp.bfloat16)
        for f in range(FRESH):
            table[cached_nodes + f] = rows[f * tokens : (f + 1) * tokens]
        for g in range(send_ref.shape[0]):
            for s in range(2):
                node = jnp.clip(pick_ref[g, 2 + s], 0, cached_nodes + FRESH - 1)
                send_ref[g, s] = table[node]


def project_fresh(pick, hidden, weight, bias, cached):
    groups = pick.shape[0]
    nodes, tokens, width = cached.shape
    block, depth = hidden[0].shape
    rows = block * len(hidden)
    step = 2048
    return pl.pallas_call(
        functools.partial(fresh_kernel, len(hidden)),
        grid=(depth // step,),
        out_shape=jax.ShapeDtypeStruct((groups, 2, tokens, width), cached.dtype),
        in_specs=[
            pl.BlockSpec(memory_space=pltpu.SMEM),
            *[pl.BlockSpec((block, step), lambda i: (0, i)) for _ in hidden],
            pl.BlockSpec((step, width), lambda i: (i, 0)),
            spec((width,)),
            spec(cached.shape),
        ],
        out_specs=spec((groups, 2, tokens, width)),
        scratch_shapes=[
            pltpu.VMEM((rows, width), jnp.float32),
            pltpu.VMEM((nodes + FRESH, tokens, width), cached.dtype),
            pltpu.VMEM((rows, step), cached.dtype),
        ],
        compiler_params=pltpu.CompilerParams(vmem_limit_bytes=SMALL_LIMIT),
        cost_estimate=pl.CostEstimate(
            flops=2 * rows * depth * width, bytes_accessed=8 * 2**20, transcendentals=0
        ),
        name="fresh",
    )(pick, *hidden, weight, bias, cached)


def take_keys(query, maximum, total, pieces, scale):
    rows = query.shape[0]
    head = query.shape[1]

    def score(c, piece):
        kv, adjust = piece
        s = lax.dot_general(
            query[c * ROWS : (c + 1) * ROWS, :],
            kv[:, :head],
            (((1,), (1,)), ((), ())),
            preferred_element_type=jnp.float32,
        )
        return s if adjust is None else adjust(s)

    def peak(s):
        top = s[:, :128]
        for k in range(1, s.shape[1] // 128):
            top = jnp.maximum(top, s[:, k * 128 : (k + 1) * 128])
        return top

    chunks = rows // ROWS
    now = [score(0, piece) for piece in pieces]
    for c in range(chunks):
        at = slice(c * ROWS, (c + 1) * ROWS)
        top = peak(now[0])
        for s in now[1:]:
            top = jnp.maximum(top, peak(s))
        old = maximum[at, :]
        new = jnp.maximum(old, jnp.max(top, axis=1, keepdims=True) * scale)
        maximum[at, :] = new
        factor = jnp.exp2(old - new)
        acc = total[at, :] * jnp.concatenate([factor, factor], axis=1)
        later = []
        for piece, s in zip(pieces, now):
            if c + 1 < chunks:
                later.append(score(c + 1, piece))
            weights = jnp.exp2(s * scale - new[:, :1]).astype(jnp.bfloat16)
            kv = piece[0]
            values = jnp.concatenate(
                [kv[:, head:], jnp.ones((kv.shape[0], head), jnp.bfloat16)], axis=1
            )
            acc = acc + jnp.dot(weights, values, preferred_element_type=jnp.float32)
        total[at, :] = acc
        now = later


def plain_pieces(ref):
    return [(ref.at[pl.ds(k, SUB), :], None) for k in range(0, ref.shape[0], SUB)]


def masked_pieces(ref, bias_ref):
    def adjust(k, s):
        bias = [bias_ref[row : row + 1, :] for row in range(k // 128, (k + SUB) // 128)]
        return s + jnp.concatenate(bias, axis=1)

    return [
        (ref.at[pl.ds(k, SUB), :], functools.partial(adjust, k))
        for k in range(0, ref.shape[0], SUB)
    ]


def own_piece(ref, steps):
    count = ref.shape[0]

    def adjust(s):
        row = lax.broadcasted_iota(jnp.int32, s.shape, 0) % count
        key = lax.broadcasted_iota(jnp.int32, s.shape, 1)
        seen = (row // steps == key // steps) & (key <= row)
        return jnp.where(seen, s, LOW)

    return [(ref.at[pl.ds(0, count), :], adjust)]


def load_query(q_ref, query):
    rows, head = q_ref.shape[0], query.shape[1]
    for j in range(q_ref.shape[1] // head):
        query[j * rows : (j + 1) * rows, :] = q_ref[:, j * head : (j + 1) * head]


def put_state(maximum, total, stat_ref, acc_ref):
    head = acc_ref.shape[1]
    lane = lax.broadcasted_iota(jnp.int32, stat_ref.shape, 1)
    stat_ref[...] = jnp.where(lane < head // 2, maximum[...], total[:, head:])
    acc_ref[...] = total[:, :head]


def get_state(stat_ref, acc_ref, maximum, total):
    rows, head = acc_ref.shape
    maximum[...] = jnp.broadcast_to(stat_ref[:, :1], (rows, head))
    total[:, :head] = acc_ref[...]
    total[:, head:] = jnp.broadcast_to(stat_ref[:, head - 1 :], (rows, head))


def first_kernel(scale, q_ref, prefix_ref, stat_ref, acc_ref, query, maximum, total):
    step = pl.program_id(0)

    @pl.when(step == 0)
    def _():
        load_query(q_ref, query)
        maximum[...] = jnp.full_like(maximum, LOW)
        total[...] = jnp.zeros_like(total)

    take_keys(query, maximum, total, plain_pieces(prefix_ref), scale)

    @pl.when(step == pl.num_programs(0) - 1)
    def _():
        put_state(maximum, total, stat_ref, acc_ref)


def middle_kernel(scale, steps, blocks, q_ref, prefix_ref, path_ref, bias_ref, own_ref, stat_in, acc_in, stat_ref, acc_ref, query, maximum, total):
    step = pl.program_id(0)

    @pl.when(step == 0)
    def _():
        load_query(q_ref, query)
        get_state(stat_in, acc_in, maximum, total)

    @pl.when(step < blocks)
    def _():
        take_keys(query, maximum, total, plain_pieces(prefix_ref), scale)

    @pl.when(step == blocks)
    def _():
        pieces = masked_pieces(path_ref, bias_ref) + own_piece(own_ref, steps)
        take_keys(query, maximum, total, pieces, scale)
        put_state(maximum, total, stat_ref, acc_ref)


def last_kernel(scale, q_ref, path_ref, bias_ref, stat_in, acc_in, out_ref, query, maximum, total):
    load_query(q_ref, query)
    get_state(stat_in, acc_in, maximum, total)
    take_keys(query, maximum, total, masked_pieces(path_ref, bias_ref), scale)
    rows, head = q_ref.shape[0], query.shape[1]
    for j in range(q_ref.shape[1] // head):
        at = slice(j * rows, (j + 1) * rows)
        out_ref[:, j * head : (j + 1) * head] = (total[at, :head] / total[at, head:]).astype(
            out_ref.dtype
        )


def attention_cost(rows, head, keys):
    return pl.CostEstimate(
        flops=8 * rows * head * keys,
        bytes_accessed=4 * keys * head,
        transcendentals=rows * keys,
    )


def per_device(
    prefix_kv,
    cached_node_states,
    fresh_hidden,
    key_value_weight,
    key_value_bias,
    decode_q,
    decoded_key_value,
    parent,
    child_parent,
    node_len,
):
    steps = 4
    head = prefix_kv.shape[2] // 2
    scale = head ** (-0.5) * LOG2E
    prefix, cached, own = prefix_kv[0], cached_node_states[0], decoded_key_value[0]
    rows = decode_q.shape[0]
    queries = rows * (decode_q.shape[1] // head)
    tp = lax.axis_size("tp")

    hidden = [fresh_hidden] + [
        lax.ppermute(fresh_hidden, "tp", [(t, t ^ k) for t in range(tp)]) for k in range(1, tp)
    ]
    pick, bias_a, bias_b, send_a = route(parent, child_parent, node_len, cached)
    path_a = lax.all_to_all(send_a, "group", 0, 0, tiled=True).reshape(-1, 2 * head)

    state = (jax.ShapeDtypeStruct((queries, head), jnp.float32),) * 2
    params = pltpu.CompilerParams(vmem_limit_bytes=VMEM_LIMIT)
    scratch = [
        pltpu.VMEM((queries, head), jnp.bfloat16),
        pltpu.VMEM((queries, head), jnp.float32),
        pltpu.VMEM((queries, 2 * head), jnp.float32),
    ]
    all_blocks = prefix.shape[0] // BLOCK
    blocks = all_blocks - FIRST_BLOCKS
    stat, acc = pl.pallas_call(
        functools.partial(first_kernel, scale),
        grid=(FIRST_BLOCKS,),
        out_shape=state,
        in_specs=[spec(decode_q.shape), pl.BlockSpec((BLOCK, 2 * head), lambda i: (i, 0))],
        out_specs=[spec(s.shape) for s in state],
        scratch_shapes=scratch,
        compiler_params=params,
        cost_estimate=attention_cost(queries, head, FIRST_BLOCKS * BLOCK),
        name="attend_first",
    )(decode_q, prefix)

    send_b = project_fresh(pick, hidden, key_value_weight, key_value_bias, cached)
    path_b = lax.all_to_all(send_b, "group", 0, 0, tiled=True).reshape(-1, 2 * head)

    stat, acc = pl.pallas_call(
        functools.partial(middle_kernel, scale, steps, blocks),
        grid=(blocks + 1,),
        out_shape=state,
        in_specs=[
            spec(decode_q.shape),
            pl.BlockSpec(
                (BLOCK, 2 * head), lambda i: (jnp.minimum(i + FIRST_BLOCKS, all_blocks - 1), 0)
            ),
            spec(path_a.shape),
            spec(bias_a.shape),
            spec(own.shape),
            spec(state[0].shape),
            spec(state[1].shape),
        ],
        out_specs=[spec(s.shape) for s in state],
        scratch_shapes=scratch,
        compiler_params=params,
        cost_estimate=attention_cost(queries, head, blocks * BLOCK + path_a.shape[0]),
        name="attend_middle",
    )(decode_q, prefix, path_a, bias_a, own, stat, acc)

    return pl.pallas_call(
        functools.partial(last_kernel, scale),
        out_shape=jax.ShapeDtypeStruct(decode_q.shape, jnp.bfloat16),
        in_specs=[spec(a.shape) for a in (decode_q, path_b, bias_b) + state],
        out_specs=spec(decode_q.shape),
        scratch_shapes=scratch,
        compiler_params=params,
        cost_estimate=attention_cost(queries, head, path_b.shape[0]),
        name="attend_last",
    )(decode_q, path_b, bias_b, stat, acc)


def solution(mesh):
    placed = (
        P("tp", None, None),
        P("tp", "group", None, None),
        P(("group", "tp"), None),
        P(None, "tp"),
        P("tp"),
        P("group", "tp"),
        P("tp", "group", None),
        P(),
        P(),
        P(),
    )

    return jax.shard_map(
        per_device, mesh=mesh, in_specs=placed, out_specs=P("group", "tp"), check_vma=False
    )
```

```python
import functools

import jax
import jax.numpy as jnp
from jax import lax
from jax.experimental import pallas as pl
from jax.experimental.pallas import tpu as pltpu
from jax.sharding import PartitionSpec as P

SLOTS = 4
FRESH = 2
SUB = 512
ROWS = 256
BLOCK = 4096
FIRST_BLOCKS = 2
LOW = -1e30
LOG2E = 1.4426950408889634
VMEM_LIMIT = 56 * 2**20
SMALL_LIMIT = 16 * 2**20


def spec(shape):
    return pl.BlockSpec(shape, lambda *_: (0,) * len(shape))


def lookup(parts, positions):
    low, high = positions & 127, positions >> 7
    result = jnp.zeros_like(positions)
    for row, part in enumerate(parts):
        table = jnp.broadcast_to(part, positions.shape)
        result = jnp.where(high == row, jnp.take_along_axis(table, low, axis=1), result)
    return result


def rows_of(table):
    return [table[row : row + 1, :] for row in range(table.shape[0])]


def ranks(flags):
    width = flags.shape[1]
    before = lax.broadcasted_iota(jnp.int32, (width, width), 0) < lax.broadcasted_iota(
        jnp.int32, (width, width), 1
    )
    return jnp.dot(
        flags.astype(jnp.bfloat16), before.astype(jnp.bfloat16), preferred_element_type=jnp.float32
    )


def slot_sums(held, values, inner, cached_nodes):
    cached = held & (inner < cached_nodes)
    fresh = held & (inner >= cached_nodes)
    rank_cached = ranks(jnp.where(cached, 1.0, 0.0))
    rank_fresh = (SLOTS - 1) - ranks(jnp.where(fresh, 1.0, 0.0))
    slot = jnp.where(cached, rank_cached, rank_fresh)
    return [
        jnp.sum(jnp.where(held & (slot == float(s)), values, 0.0), axis=1, keepdims=True)
        for s in range(SLOTS)
    ]


def route_kernel(groups, parent_ref, child_ref, len_ref, cached_ref, pick_ref, bias_a_ref, bias_b_ref, send_ref, pick_v, pick_s, sem):
    me = lax.axis_index("group")
    cached_nodes = cached_ref.shape[0]
    per_node = cached_nodes + FRESH
    width = 128
    parent = parent_ref[...]
    none = parent.shape[0] * 128
    jump = jnp.where(parent < 0, none, parent)
    lane = lax.broadcasted_iota(jnp.int32, (groups, width), 1)
    group_row = lax.broadcasted_iota(jnp.int32, (groups, width), 0)
    path = jnp.full((groups, width), none, jnp.int32)
    for g in range(groups):
        path = jnp.where((lane == 0) & (group_row == g), child_ref[g], path)
    reach = 1
    while reach < 64:
        tables = rows_of(jump)
        ahead = jnp.where(path < none, lookup(tables, jnp.minimum(path, none - 1)), none)
        path = jnp.where((lane >= reach) & (lane < 2 * reach), pltpu.roll(ahead, reach, 1), path)
        jump = jnp.where(jump < none, lookup(tables, jnp.minimum(jump, none - 1)), none)
        reach *= 2
    inner = path % per_node
    there = path < none
    picks = slot_sums(
        there & (path // per_node == me), inner.astype(jnp.float32), inner, cached_nodes
    )
    pick = jnp.zeros((groups, width), jnp.float32)
    for s in range(SLOTS):
        pick = jnp.where(lane == s, picks[s], pick)
    pick = pick.astype(jnp.int32)
    pick_v[...] = pick
    pick_ref[...] = pick
    copy = pltpu.make_async_copy(pick_v, pick_s, sem)
    copy.start()
    mine = jnp.sum(jnp.where(group_row == me, path, 0).astype(jnp.float32), axis=0, keepdims=True)
    mine = jnp.broadcast_to(mine, (groups, width)).astype(jnp.int32)
    there = mine < none
    lengths = lookup(rows_of(len_ref[...]), jnp.minimum(mine, none - 1)).astype(jnp.float32)
    valid = slot_sums(
        there & (mine // per_node == group_row), lengths, mine % per_node, cached_nodes
    )
    half = width // 2
    token = (lane % half).astype(jnp.float32)
    for ref, first in ((bias_a_ref, 0), (bias_b_ref, 2)):
        limit = jnp.where(lane < half, valid[first], valid[first + 1])
        ref[...] = jnp.where(token < limit, 0.0, LOW)
    copy.wait()
    for g in range(groups):
        for s in range(2):
            node = jnp.minimum(pick_s[g, s], cached_nodes - 1)
            send_ref[g, s] = cached_ref[node]


def route(parent, child_parent, node_len, cached):
    groups = child_parent.shape[0]
    _, tokens, width = cached.shape
    rows = parent.shape[0] // 128
    table = jax.ShapeDtypeStruct((groups, 128), jnp.int32)
    bias = jax.ShapeDtypeStruct((groups, 128), jnp.float32)
    out = (table, bias, bias, jax.ShapeDtypeStruct((groups, 2, tokens, width), cached.dtype))
    args = (
        parent.reshape(rows, 128),
        child_parent,
        node_len.reshape(rows, 128),
        cached,
    )
    return pl.pallas_call(
        functools.partial(route_kernel, groups),
        out_shape=out,
        in_specs=[
            spec(args[0].shape),
            pl.BlockSpec(memory_space=pltpu.SMEM),
            spec(args[2].shape),
            spec(args[3].shape),
        ],
        out_specs=[spec(o.shape) for o in out],
        scratch_shapes=[
            pltpu.VMEM((groups, 128), jnp.int32),
            pltpu.SMEM((groups, 128), jnp.int32),
            pltpu.SemaphoreType.DMA,
        ],
        cost_estimate=pl.CostEstimate(flops=2**24, bytes_accessed=2**21, transcendentals=0),
        name="route",
    )(*args)


def fresh_kernel(parts, pick_ref, *refs):
    hidden_refs = refs[:parts]
    weight_ref, bias_ref, cached_ref, send_ref, total, table, hidden = refs[parts:]
    step = pl.program_id(0)
    me = lax.axis_index("tp")
    cached_nodes, tokens, _ = cached_ref.shape

    @pl.when(step == 0)
    def _():
        total[...] = jnp.zeros_like(total)
        table[:cached_nodes] = cached_ref[...]

    for k, ref in enumerate(hidden_refs):
        block = ref.shape[0]
        hidden[pl.ds(pl.multiple_of((me ^ k) * block, block), block), :] = ref[...]
    total[...] += jnp.dot(hidden[...], weight_ref[...], preferred_element_type=jnp.float32)

    @pl.when(step == pl.num_programs(0) - 1)
    def _():
        rows = (total[...] + bias_ref[...].astype(jnp.float32)[None, :]).astype(jnp.bfloat16)
        for f in range(FRESH):
            table[cached_nodes + f] = rows[f * tokens : (f + 1) * tokens]
        for g in range(send_ref.shape[0]):
            for s in range(2):
                node = jnp.clip(pick_ref[g, 2 + s], 0, cached_nodes + FRESH - 1)
                send_ref[g, s] = table[node]


def project_fresh(pick, hidden, weight, bias, cached):
    groups = pick.shape[0]
    nodes, tokens, width = cached.shape
    block, depth = hidden[0].shape
    rows = block * len(hidden)
    step = 2048
    return pl.pallas_call(
        functools.partial(fresh_kernel, len(hidden)),
        grid=(depth // step,),
        out_shape=jax.ShapeDtypeStruct((groups, 2, tokens, width), cached.dtype),
        in_specs=[
            pl.BlockSpec(memory_space=pltpu.SMEM),
            *[pl.BlockSpec((block, step), lambda i: (0, i)) for _ in hidden],
            pl.BlockSpec((step, width), lambda i: (i, 0)),
            spec((width,)),
            spec(cached.shape),
        ],
        out_specs=spec((groups, 2, tokens, width)),
        scratch_shapes=[
            pltpu.VMEM((rows, width), jnp.float32),
            pltpu.VMEM((nodes + FRESH, tokens, width), cached.dtype),
            pltpu.VMEM((rows, step), cached.dtype),
        ],
        compiler_params=pltpu.CompilerParams(vmem_limit_bytes=SMALL_LIMIT),
        cost_estimate=pl.CostEstimate(
            flops=2 * rows * depth * width, bytes_accessed=8 * 2**20, transcendentals=0
        ),
        name="fresh",
    )(pick, *hidden, weight, bias, cached)


def take_keys(query, maximum, total, pieces, scale):
    rows = query.shape[0]
    head = query.shape[1]

    def score(c, piece):
        kv, adjust = piece
        s = lax.dot_general(
            query[c * ROWS : (c + 1) * ROWS, :],
            kv[:, :head],
            (((1,), (1,)), ((), ())),
            preferred_element_type=jnp.float32,
        )
        return s if adjust is None else adjust(s)

    def peak(s):
        top = s[:, :128]
        for k in range(1, s.shape[1] // 128):
            top = jnp.maximum(top, s[:, k * 128 : (k + 1) * 128])
        return top

    chunks = rows // ROWS
    now = [score(0, piece) for piece in pieces]
    for c in range(chunks):
        at = slice(c * ROWS, (c + 1) * ROWS)
        top = peak(now[0])
        for s in now[1:]:
            top = jnp.maximum(top, peak(s))
        old = maximum[at, :]
        new = jnp.maximum(old, jnp.max(top, axis=1, keepdims=True) * scale)
        maximum[at, :] = new
        factor = jnp.exp2(old - new)
        acc = total[at, :] * jnp.concatenate([factor, factor], axis=1)
        later = []
        for piece, s in zip(pieces, now):
            if c + 1 < chunks:
                later.append(score(c + 1, piece))
            weights = jnp.exp2(s * scale - new[:, :1]).astype(jnp.bfloat16)
            kv = piece[0]
            values = jnp.concatenate(
                [kv[:, head:], jnp.ones((kv.shape[0], head), jnp.bfloat16)], axis=1
            )
            acc = acc + jnp.dot(weights, values, preferred_element_type=jnp.float32)
        total[at, :] = acc
        now = later


def plain_pieces(ref):
    return [(ref.at[pl.ds(k, SUB), :], None) for k in range(0, ref.shape[0], SUB)]


def masked_pieces(ref, bias_ref):
    def adjust(k, s):
        bias = [bias_ref[row : row + 1, :] for row in range(k // 128, (k + SUB) // 128)]
        return s + jnp.concatenate(bias, axis=1)

    return [
        (ref.at[pl.ds(k, SUB), :], functools.partial(adjust, k))
        for k in range(0, ref.shape[0], SUB)
    ]


def own_piece(ref, steps):
    count = ref.shape[0]

    def adjust(s):
        row = lax.broadcasted_iota(jnp.int32, s.shape, 0) % count
        key = lax.broadcasted_iota(jnp.int32, s.shape, 1)
        seen = (row // steps == key // steps) & (key <= row)
        return jnp.where(seen, s, LOW)

    return [(ref.at[pl.ds(0, count), :], adjust)]


def load_query(q_ref, query):
    rows, head = q_ref.shape[0], query.shape[1]
    for j in range(q_ref.shape[1] // head):
        query[j * rows : (j + 1) * rows, :] = q_ref[:, j * head : (j + 1) * head]


def put_state(maximum, total, stat_ref, acc_ref):
    head = acc_ref.shape[1]
    lane = lax.broadcasted_iota(jnp.int32, stat_ref.shape, 1)
    stat_ref[...] = jnp.where(lane < head // 2, maximum[...], total[:, head:])
    acc_ref[...] = total[:, :head]


def get_state(stat_ref, acc_ref, maximum, total):
    rows, head = acc_ref.shape
    maximum[...] = jnp.broadcast_to(stat_ref[:, :1], (rows, head))
    total[:, :head] = acc_ref[...]
    total[:, head:] = jnp.broadcast_to(stat_ref[:, head - 1 :], (rows, head))


def first_kernel(scale, q_ref, prefix_ref, stat_ref, acc_ref, query, maximum, total):
    step = pl.program_id(0)

    @pl.when(step == 0)
    def _():
        load_query(q_ref, query)
        maximum[...] = jnp.full_like(maximum, LOW)
        total[...] = jnp.zeros_like(total)

    take_keys(query, maximum, total, plain_pieces(prefix_ref), scale)

    @pl.when(step == pl.num_programs(0) - 1)
    def _():
        put_state(maximum, total, stat_ref, acc_ref)


def middle_kernel(scale, steps, blocks, q_ref, prefix_ref, path_ref, bias_ref, own_ref, stat_in, acc_in, stat_ref, acc_ref, query, maximum, total):
    step = pl.program_id(0)

    @pl.when(step == 0)
    def _():
        load_query(q_ref, query)
        get_state(stat_in, acc_in, maximum, total)

    @pl.when(step < blocks)
    def _():
        take_keys(query, maximum, total, plain_pieces(prefix_ref), scale)

    @pl.when(step == blocks)
    def _():
        pieces = masked_pieces(path_ref, bias_ref) + own_piece(own_ref, steps)
        take_keys(query, maximum, total, pieces, scale)
        put_state(maximum, total, stat_ref, acc_ref)


def last_kernel(scale, q_ref, path_ref, bias_ref, stat_in, acc_in, out_ref, query, maximum, total):
    load_query(q_ref, query)
    get_state(stat_in, acc_in, maximum, total)
    take_keys(query, maximum, total, masked_pieces(path_ref, bias_ref), scale)
    rows, head = q_ref.shape[0], query.shape[1]
    for j in range(q_ref.shape[1] // head):
        at = slice(j * rows, (j + 1) * rows)
        out_ref[:, j * head : (j + 1) * head] = (total[at, :head] / total[at, head:]).astype(
            out_ref.dtype
        )


def attention_cost(rows, head, keys):
    return pl.CostEstimate(
        flops=8 * rows * head * keys,
        bytes_accessed=4 * keys * head,
        transcendentals=rows * keys,
    )


def per_device(
    prefix_kv,
    cached_node_states,
    fresh_hidden,
    key_value_weight,
    key_value_bias,
    decode_q,
    decoded_key_value,
    parent,
    child_parent,
    node_len,
):
    steps = 4
    head = prefix_kv.shape[2] // 2
    scale = head ** (-0.5) * LOG2E
    prefix, cached, own = prefix_kv[0], cached_node_states[0], decoded_key_value[0]
    rows = decode_q.shape[0]
    queries = rows * (decode_q.shape[1] // head)
    tp = lax.axis_size("tp")

    hidden = [fresh_hidden] + [
        lax.ppermute(fresh_hidden, "tp", [(t, t ^ k) for t in range(tp)]) for k in range(1, tp)
    ]
    pick, bias_a, bias_b, send_a = route(parent, child_parent, node_len, cached)
    path_a = lax.all_to_all(send_a, "group", 0, 0, tiled=True).reshape(-1, 2 * head)

    state = (jax.ShapeDtypeStruct((queries, head), jnp.float32),) * 2
    params = pltpu.CompilerParams(vmem_limit_bytes=VMEM_LIMIT)
    scratch = [
        pltpu.VMEM((queries, head), jnp.bfloat16),
        pltpu.VMEM((queries, head), jnp.float32),
        pltpu.VMEM((queries, 2 * head), jnp.float32),
    ]
    prefix = pltpu.with_memory_space_constraint(prefix, pltpu.HBM)
    all_blocks = prefix.shape[0] // BLOCK
    blocks = all_blocks - FIRST_BLOCKS
    stat, acc = pl.pallas_call(
        functools.partial(first_kernel, scale),
        grid=(FIRST_BLOCKS,),
        out_shape=state,
        in_specs=[spec(decode_q.shape), pl.BlockSpec((BLOCK, 2 * head), lambda i: (i, 0))],
        out_specs=[spec(s.shape) for s in state],
        scratch_shapes=scratch,
        compiler_params=params,
        cost_estimate=attention_cost(queries, head, FIRST_BLOCKS * BLOCK),
        name="attend_first",
    )(decode_q, prefix)

    send_b = project_fresh(pick, hidden, key_value_weight, key_value_bias, cached)
    path_b = lax.all_to_all(send_b, "group", 0, 0, tiled=True).reshape(-1, 2 * head)
    path_b = pltpu.with_memory_space_constraint(path_b, pltpu.VMEM)

    stat, acc = pl.pallas_call(
        functools.partial(middle_kernel, scale, steps, blocks),
        grid=(blocks + 1,),
        out_shape=state,
        in_specs=[
            spec(decode_q.shape),
            pl.BlockSpec(
                (BLOCK, 2 * head), lambda i: (jnp.minimum(i + FIRST_BLOCKS, all_blocks - 1), 0)
            ),
            spec(path_a.shape),
            spec(bias_a.shape),
            spec(own.shape),
            spec(state[0].shape),
            spec(state[1].shape),
        ],
        out_specs=[spec(s.shape) for s in state],
        scratch_shapes=scratch,
        compiler_params=params,
        cost_estimate=attention_cost(queries, head, blocks * BLOCK + path_a.shape[0]),
        name="attend_middle",
    )(decode_q, prefix, path_a, bias_a, own, stat, acc)

    return pl.pallas_call(
        functools.partial(last_kernel, scale),
        out_shape=jax.ShapeDtypeStruct(decode_q.shape, jnp.bfloat16),
        in_specs=[
            spec(decode_q.shape),
            pl.BlockSpec(memory_space=pltpu.VMEM),
            spec(bias_b.shape),
            spec(state[0].shape),
            spec(state[1].shape),
        ],
        out_specs=spec(decode_q.shape),
        scratch_shapes=scratch,
        compiler_params=params,
        cost_estimate=attention_cost(queries, head, path_b.shape[0]),
        name="attend_last",
    )(decode_q, path_b, bias_b, stat, acc)


def solution(mesh):
    placed = (
        P("tp", None, None),
        P("tp", "group", None, None),
        P(("group", "tp"), None),
        P(None, "tp"),
        P("tp"),
        P("group", "tp"),
        P("tp", "group", None),
        P(),
        P(),
        P(),
    )

    return jax.shard_map(
        per_device, mesh=mesh, in_specs=placed, out_specs=P("group", "tp"), check_vma=False
    )
```

```python
import functools

import jax
import jax.numpy as jnp
from jax import lax
from jax.experimental import pallas as pl
from jax.experimental.pallas import tpu as pltpu
from jax.sharding import PartitionSpec as P

SLOTS = 4
FRESH = 2
SUB = 512
ROWS = 256
BLOCK = 4096
FIRST_BLOCKS = 2
LOW = -1e30
LOG2E = 1.4426950408889634
VMEM_LIMIT = 56 * 2**20
SMALL_LIMIT = 16 * 2**20


def spec(shape):
    return pl.BlockSpec(shape, lambda *_: (0,) * len(shape))


def lookup(parts, positions):
    low, high = positions & 127, positions >> 7
    result = jnp.zeros_like(positions)
    for row, part in enumerate(parts):
        table = jnp.broadcast_to(part, positions.shape)
        result = jnp.where(high == row, jnp.take_along_axis(table, low, axis=1), result)
    return result


def rows_of(table):
    return [table[row : row + 1, :] for row in range(table.shape[0])]


def ranks(flags):
    width = flags.shape[1]
    before = lax.broadcasted_iota(jnp.int32, (width, width), 0) < lax.broadcasted_iota(
        jnp.int32, (width, width), 1
    )
    return jnp.dot(
        flags.astype(jnp.bfloat16), before.astype(jnp.bfloat16), preferred_element_type=jnp.float32
    )


def slot_sums(held, values, inner, cached_nodes):
    cached = held & (inner < cached_nodes)
    fresh = held & (inner >= cached_nodes)
    rank_cached = ranks(jnp.where(cached, 1.0, 0.0))
    rank_fresh = (SLOTS - 1) - ranks(jnp.where(fresh, 1.0, 0.0))
    slot = jnp.where(cached, rank_cached, rank_fresh)
    return [
        jnp.sum(jnp.where(held & (slot == float(s)), values, 0.0), axis=1, keepdims=True)
        for s in range(SLOTS)
    ]


def route_kernel(groups, parent_ref, child_ref, len_ref, cached_ref, pick_ref, bias_a_ref, bias_b_ref, send_ref, pick_v, pick_s, cached_v, sem):
    me = lax.axis_index("group")
    cached_nodes = cached_ref.shape[0]
    fetch = pltpu.make_async_copy(cached_ref, cached_v, sem.at[1])
    fetch.start()
    per_node = cached_nodes + FRESH
    width = 128
    parent = parent_ref[...]
    none = parent.shape[0] * 128
    jump = jnp.where(parent < 0, none, parent)
    lane = lax.broadcasted_iota(jnp.int32, (groups, width), 1)
    group_row = lax.broadcasted_iota(jnp.int32, (groups, width), 0)
    path = jnp.full((groups, width), none, jnp.int32)
    for g in range(groups):
        path = jnp.where((lane == 0) & (group_row == g), child_ref[g], path)
    reach = 1
    while reach < 64:
        tables = rows_of(jump)
        ahead = jnp.where(path < none, lookup(tables, jnp.minimum(path, none - 1)), none)
        path = jnp.where((lane >= reach) & (lane < 2 * reach), pltpu.roll(ahead, reach, 1), path)
        reach *= 2
        if reach < 64:
            jump = jnp.where(jump < none, lookup(tables, jnp.minimum(jump, none - 1)), none)
    inner = path % per_node
    there = path < none
    picks = slot_sums(
        there & (path // per_node == me), inner.astype(jnp.float32), inner, cached_nodes
    )
    pick = jnp.zeros((groups, width), jnp.float32)
    for s in range(SLOTS):
        pick = jnp.where(lane == s, picks[s], pick)
    pick = pick.astype(jnp.int32)
    pick_v[...] = pick
    pick_ref[...] = pick
    copy = pltpu.make_async_copy(pick_v, pick_s, sem.at[0])
    copy.start()
    mine = jnp.sum(jnp.where(group_row == me, path, 0).astype(jnp.float32), axis=0, keepdims=True)
    mine = jnp.broadcast_to(mine, (groups, width)).astype(jnp.int32)
    there = mine < none
    lengths = lookup(rows_of(len_ref[...]), jnp.minimum(mine, none - 1)).astype(jnp.float32)
    valid = slot_sums(
        there & (mine // per_node == group_row), lengths, mine % per_node, cached_nodes
    )
    half = width // 2
    token = (lane % half).astype(jnp.float32)
    for ref, first in ((bias_a_ref, 0), (bias_b_ref, 2)):
        limit = jnp.where(lane < half, valid[first], valid[first + 1])
        ref[...] = jnp.where(token < limit, 0.0, LOW)
    copy.wait()
    fetch.wait()
    for g in range(groups):
        for s in range(2):
            node = jnp.minimum(pick_s[g, s], cached_nodes - 1)
            send_ref[g, s] = cached_v[node]


def route(parent, child_parent, node_len, cached):
    groups = child_parent.shape[0]
    _, tokens, width = cached.shape
    rows = parent.shape[0] // 128
    table = jax.ShapeDtypeStruct((groups, 128), jnp.int32)
    bias = jax.ShapeDtypeStruct((groups, 128), jnp.float32)
    out = (table, bias, bias, jax.ShapeDtypeStruct((groups, 2, tokens, width), cached.dtype))
    args = (
        parent.reshape(rows, 128),
        child_parent,
        node_len.reshape(rows, 128),
        pltpu.with_memory_space_constraint(cached, pltpu.HBM),
    )
    return pl.pallas_call(
        functools.partial(route_kernel, groups),
        out_shape=out,
        in_specs=[
            spec(args[0].shape),
            pl.BlockSpec(memory_space=pltpu.SMEM),
            spec(args[2].shape),
            pl.BlockSpec(memory_space=pl.ANY),
        ],
        out_specs=[spec(o.shape) for o in out],
        scratch_shapes=[
            pltpu.VMEM((groups, 128), jnp.int32),
            pltpu.SMEM((groups, 128), jnp.int32),
            pltpu.VMEM(cached.shape, cached.dtype),
            pltpu.SemaphoreType.DMA((2,)),
        ],
        cost_estimate=pl.CostEstimate(flops=2**24, bytes_accessed=2**21, transcendentals=0),
        name="route",
    )(*args)


def fresh_kernel(parts, pick_ref, *refs):
    hidden_refs = refs[:parts]
    weight_ref, bias_ref, cached_ref, send_ref, table, hidden = refs[parts:]
    cached_nodes, tokens, _ = cached_ref.shape
    me = lax.axis_index("tp")
    for k, ref in enumerate(hidden_refs):
        block = ref.shape[0]
        hidden[pl.ds(pl.multiple_of((me ^ k) * block, block), block), :] = ref[...]
    table[:cached_nodes] = cached_ref[...]
    total = jnp.dot(hidden[...], weight_ref[...], preferred_element_type=jnp.float32)
    rows = (total + bias_ref[...].astype(jnp.float32)[None, :]).astype(jnp.bfloat16)
    for f in range(FRESH):
        table[cached_nodes + f] = rows[f * tokens : (f + 1) * tokens]
    for g in range(send_ref.shape[0]):
        for s in range(2):
            node = jnp.clip(pick_ref[g, 2 + s], 0, cached_nodes + FRESH - 1)
            send_ref[g, s] = table[node]


def project_fresh(pick, hidden, weight, bias, cached):
    groups = pick.shape[0]
    nodes, tokens, width = cached.shape
    block, depth = hidden[0].shape
    rows = block * len(hidden)
    on_chip = pl.BlockSpec(memory_space=pltpu.VMEM)
    return pl.pallas_call(
        functools.partial(fresh_kernel, len(hidden)),
        out_shape=jax.ShapeDtypeStruct((groups, 2, tokens, width), cached.dtype),
        in_specs=[pl.BlockSpec(memory_space=pltpu.SMEM)] + [on_chip] * (len(hidden) + 3),
        out_specs=spec((groups, 2, tokens, width)),
        scratch_shapes=[
            pltpu.VMEM((nodes + FRESH, tokens, width), cached.dtype),
            pltpu.VMEM((rows, depth), cached.dtype),
        ],
        compiler_params=pltpu.CompilerParams(vmem_limit_bytes=SMALL_LIMIT),
        cost_estimate=pl.CostEstimate(
            flops=2 * rows * depth * width, bytes_accessed=8 * 2**20, transcendentals=0
        ),
        name="fresh",
    )(pick, *hidden, weight, bias, cached)


def take_keys(query, maximum, total, pieces, scale):
    rows = query.shape[0]
    head = query.shape[1]

    def score(c, piece):
        kv, adjust = piece
        s = lax.dot_general(
            query[c * ROWS : (c + 1) * ROWS, :],
            kv[:, :head],
            (((1,), (1,)), ((), ())),
            preferred_element_type=jnp.float32,
        )
        return s if adjust is None else adjust(s)

    def peak(s):
        top = s[:, :128]
        for k in range(1, s.shape[1] // 128):
            top = jnp.maximum(top, s[:, k * 128 : (k + 1) * 128])
        return top

    chunks = rows // ROWS
    now = [score(0, piece) for piece in pieces]
    for c in range(chunks):
        at = slice(c * ROWS, (c + 1) * ROWS)
        top = peak(now[0])
        for s in now[1:]:
            top = jnp.maximum(top, peak(s))
        old = maximum[at, :]
        new = jnp.maximum(old, jnp.max(top, axis=1, keepdims=True) * scale)
        maximum[at, :] = new
        factor = jnp.exp2(old - new)
        acc = total[at, :] * jnp.concatenate([factor, factor], axis=1)
        later = []
        for piece, s in zip(pieces, now):
            if c + 1 < chunks:
                later.append(score(c + 1, piece))
            weights = jnp.exp2(s * scale - new[:, :1]).astype(jnp.bfloat16)
            kv = piece[0]
            values = jnp.concatenate(
                [kv[:, head:], jnp.ones((kv.shape[0], head), jnp.bfloat16)], axis=1
            )
            acc = acc + jnp.dot(weights, values, preferred_element_type=jnp.float32)
        total[at, :] = acc
        now = later


def plain_pieces(ref):
    return [(ref.at[pl.ds(k, SUB), :], None) for k in range(0, ref.shape[0], SUB)]


def masked_pieces(ref, bias_ref):
    def adjust(k, s):
        bias = [bias_ref[row : row + 1, :] for row in range(k // 128, (k + SUB) // 128)]
        return s + jnp.concatenate(bias, axis=1)

    return [
        (ref.at[pl.ds(k, SUB), :], functools.partial(adjust, k))
        for k in range(0, ref.shape[0], SUB)
    ]


def own_piece(ref, steps):
    count = ref.shape[0]

    def adjust(s):
        row = lax.broadcasted_iota(jnp.int32, s.shape, 0) % count
        key = lax.broadcasted_iota(jnp.int32, s.shape, 1)
        seen = (row // steps == key // steps) & (key <= row)
        return jnp.where(seen, s, LOW)

    return [(ref.at[pl.ds(0, count), :], adjust)]


def load_query(q_ref, query):
    rows, head = q_ref.shape[0], query.shape[1]
    for j in range(q_ref.shape[1] // head):
        query[j * rows : (j + 1) * rows, :] = q_ref[:, j * head : (j + 1) * head]


def put_state(maximum, total, stat_ref, acc_ref):
    head = acc_ref.shape[1]
    lane = lax.broadcasted_iota(jnp.int32, stat_ref.shape, 1)
    stat_ref[...] = jnp.where(lane < head // 2, maximum[...], total[:, head:])
    acc_ref[...] = total[:, :head]


def get_state(stat_ref, acc_ref, maximum, total):
    rows, head = acc_ref.shape
    maximum[...] = jnp.broadcast_to(stat_ref[:, :1], (rows, head))
    total[:, :head] = acc_ref[...]
    total[:, head:] = jnp.broadcast_to(stat_ref[:, head - 1 :], (rows, head))


def merge_state(stat_ref, acc_ref, maximum, total):
    rows, head = acc_ref.shape
    old = jnp.broadcast_to(stat_ref[:, :1], (rows, head))
    summed = jnp.broadcast_to(stat_ref[:, head - 1 :], (rows, head))
    new = jnp.maximum(old, maximum[...])
    theirs, ours = jnp.exp2(old - new), jnp.exp2(maximum[...] - new)
    maximum[...] = new
    total[:, :head] = total[:, :head] * ours + acc_ref[...] * theirs
    total[:, head:] = total[:, head:] * ours + summed * theirs


def empty_state(maximum, total):
    maximum[...] = jnp.full_like(maximum, LOW)
    total[...] = jnp.zeros_like(total)


def first_kernel(scale, q_ref, prefix_ref, stat_ref, acc_ref, query, maximum, total):
    step = pl.program_id(0)

    @pl.when(step == 0)
    def _():
        load_query(q_ref, query)
        empty_state(maximum, total)

    take_keys(query, maximum, total, plain_pieces(prefix_ref), scale)

    @pl.when(step == pl.num_programs(0) - 1)
    def _():
        put_state(maximum, total, stat_ref, acc_ref)


def middle_kernel(scale, steps, blocks, q_ref, prefix_ref, path_ref, bias_ref, own_ref, stat_in, acc_in, stat_ref, acc_ref, query, maximum, total, stat_v, acc_v, path_v, sem):
    step = pl.program_id(0)
    pairs = ((path_ref, path_v), (stat_in, stat_v), (acc_in, acc_v))
    copies = [pltpu.make_async_copy(a, b, sem.at[k]) for k, (a, b) in enumerate(pairs)]

    @pl.when(step == 0)
    def _():
        for copy in copies:
            copy.start()
        load_query(q_ref, query)
        empty_state(maximum, total)

    @pl.when(step < blocks)
    def _():
        take_keys(query, maximum, total, plain_pieces(prefix_ref), scale)

    @pl.when(step == blocks)
    def _():
        for copy in copies:
            copy.wait()
        pieces = masked_pieces(path_v, bias_ref) + own_piece(own_ref, steps)
        take_keys(query, maximum, total, pieces, scale)
        merge_state(stat_v, acc_v, maximum, total)
        put_state(maximum, total, stat_ref, acc_ref)


def last_kernel(scale, q_ref, path_ref, bias_ref, stat_in, acc_in, out_ref, query, maximum, total):
    load_query(q_ref, query)
    get_state(stat_in, acc_in, maximum, total)
    take_keys(query, maximum, total, masked_pieces(path_ref, bias_ref), scale)
    rows, head = q_ref.shape[0], query.shape[1]
    for j in range(q_ref.shape[1] // head):
        at = slice(j * rows, (j + 1) * rows)
        out_ref[:, j * head : (j + 1) * head] = (total[at, :head] / total[at, head:]).astype(
            out_ref.dtype
        )


def attention_cost(rows, head, keys):
    return pl.CostEstimate(
        flops=8 * rows * head * keys,
        bytes_accessed=4 * keys * head,
        transcendentals=rows * keys,
    )


def per_device(
    prefix_kv,
    cached_node_states,
    fresh_hidden,
    key_value_weight,
    key_value_bias,
    decode_q,
    decoded_key_value,
    parent,
    child_parent,
    node_len,
):
    steps = 4
    head = prefix_kv.shape[2] // 2
    scale = head ** (-0.5) * LOG2E
    prefix, cached, own = prefix_kv[0], cached_node_states[0], decoded_key_value[0]
    rows = decode_q.shape[0]
    queries = rows * (decode_q.shape[1] // head)
    tp = lax.axis_size("tp")

    def moved(block, distance):
        return lax.ppermute(block, "tp", [(t, t ^ distance) for t in range(tp)])

    hidden = [fresh_hidden] * tp
    for k in (1, 2, 4, 5):
        hidden[k] = moved(fresh_hidden, k)
    hidden[6] = moved(fresh_hidden, 6)
    hidden[7] = moved(hidden[1], 6)
    hidden[3] = moved(hidden[1], 2)
    pick, bias_a, bias_b, send_a = route(parent, child_parent, node_len, cached)
    path_a = lax.all_to_all(send_a, "group", 0, 0, tiled=True).reshape(-1, 2 * head)

    state = (jax.ShapeDtypeStruct((queries, head), jnp.float32),) * 2
    params = pltpu.CompilerParams(vmem_limit_bytes=VMEM_LIMIT)
    scratch = [
        pltpu.VMEM((queries, head), jnp.bfloat16),
        pltpu.VMEM((queries, head), jnp.float32),
        pltpu.VMEM((queries, 2 * head), jnp.float32),
    ]
    prefix = pltpu.with_memory_space_constraint(prefix, pltpu.HBM)
    all_blocks = prefix.shape[0] // BLOCK
    blocks = all_blocks - FIRST_BLOCKS
    anywhere = pl.BlockSpec(memory_space=pl.ANY)
    state_scratch = [pltpu.VMEM(s.shape, s.dtype) for s in state]
    stat, acc = pl.pallas_call(
        functools.partial(first_kernel, scale),
        grid=(FIRST_BLOCKS,),
        out_shape=state,
        in_specs=[spec(decode_q.shape), pl.BlockSpec((BLOCK, 2 * head), lambda i: (i, 0))],
        out_specs=[spec(s.shape) for s in state],
        scratch_shapes=scratch,
        compiler_params=params,
        cost_estimate=attention_cost(queries, head, FIRST_BLOCKS * BLOCK),
        name="attend_first",
    )(decode_q, prefix)

    send_b = project_fresh(pick, hidden, key_value_weight, key_value_bias, cached)
    path_b = lax.all_to_all(send_b, "group", 0, 0, tiled=True).reshape(-1, 2 * head)
    path_a = pltpu.with_memory_space_constraint(path_a, pltpu.HBM)
    path_b = pltpu.with_memory_space_constraint(path_b, pltpu.VMEM)
    stat, acc = (pltpu.with_memory_space_constraint(a, pltpu.HBM) for a in (stat, acc))

    stat, acc = pl.pallas_call(
        functools.partial(middle_kernel, scale, steps, blocks),
        grid=(blocks + 1,),
        out_shape=state,
        in_specs=[
            spec(decode_q.shape),
            pl.BlockSpec(
                (BLOCK, 2 * head), lambda i: (jnp.minimum(i + FIRST_BLOCKS, all_blocks - 1), 0)
            ),
            anywhere,
            spec(bias_a.shape),
            spec(own.shape),
            anywhere,
            anywhere,
        ],
        out_specs=[spec(s.shape) for s in state],
        scratch_shapes=scratch
        + state_scratch
        + [pltpu.VMEM(path_a.shape, path_a.dtype), pltpu.SemaphoreType.DMA((3,))],
        compiler_params=params,
        cost_estimate=attention_cost(queries, head, blocks * BLOCK + path_a.shape[0]),
        name="attend_middle",
    )(decode_q, prefix, path_a, bias_a, own, stat, acc)

    return pl.pallas_call(
        functools.partial(last_kernel, scale),
        out_shape=jax.ShapeDtypeStruct(decode_q.shape, jnp.bfloat16),
        in_specs=[
            spec(decode_q.shape),
            pl.BlockSpec(memory_space=pltpu.VMEM),
            spec(bias_b.shape),
            spec(state[0].shape),
            spec(state[1].shape),
        ],
        out_specs=spec(decode_q.shape),
        scratch_shapes=scratch,
        compiler_params=params,
        cost_estimate=attention_cost(queries, head, path_b.shape[0]),
        name="attend_last",
    )(decode_q, path_b, bias_b, stat, acc)


def solution(mesh):
    placed = (
        P("tp", None, None),
        P("tp", "group", None, None),
        P(("group", "tp"), None),
        P(None, "tp"),
        P("tp"),
        P("group", "tp"),
        P("tp", "group", None),
        P(),
        P(),
        P(),
    )

    return jax.shard_map(
        per_device, mesh=mesh, in_specs=placed, out_specs=P("group", "tp"), check_vma=False
    )
```

```python
import functools

import jax
import jax.numpy as jnp
from jax import lax
from jax.experimental import pallas as pl
from jax.experimental.pallas import tpu as pltpu
from jax.sharding import PartitionSpec as P

SLOTS = 4
FRESH = 2
SUB = 512
ROWS = 256
PART = 2048
FIRST_PARTS = 3
MIDDLE_STEPS = 2
LOW = -1e30
LOG2E = 1.4426950408889634
VMEM_LIMIT = 56 * 2**20
SMALL_LIMIT = 16 * 2**20


def spec(shape):
    return pl.BlockSpec(shape, lambda *_: (0,) * len(shape))


def lookup(parts, positions):
    low, high = positions & 127, positions >> 7
    result = jnp.zeros_like(positions)
    for row, part in enumerate(parts):
        table = jnp.broadcast_to(part, positions.shape)
        result = jnp.where(high == row, jnp.take_along_axis(table, low, axis=1), result)
    return result


def rows_of(table):
    return [table[row : row + 1, :] for row in range(table.shape[0])]


def ranks(flags):
    width = flags.shape[1]
    before = lax.broadcasted_iota(jnp.int32, (width, width), 0) < lax.broadcasted_iota(
        jnp.int32, (width, width), 1
    )
    return jnp.dot(
        flags.astype(jnp.bfloat16), before.astype(jnp.bfloat16), preferred_element_type=jnp.float32
    )


def slot_sums(held, values, inner, cached_nodes):
    cached = held & (inner < cached_nodes)
    fresh = held & (inner >= cached_nodes)
    rank_cached = ranks(jnp.where(cached, 1.0, 0.0))
    rank_fresh = (SLOTS - 1) - ranks(jnp.where(fresh, 1.0, 0.0))
    slot = jnp.where(cached, rank_cached, rank_fresh)
    return [
        jnp.sum(jnp.where(held & (slot == float(s)), values, 0.0), axis=1, keepdims=True)
        for s in range(SLOTS)
    ]


def route_kernel(groups, parent_ref, child_ref, len_ref, cached_ref, pick_ref, bias_a_ref, bias_b_ref, send_ref, pick_v, pick_s, cached_v, sem):
    me = lax.axis_index("group")
    cached_nodes = cached_ref.shape[0]
    fetch = pltpu.make_async_copy(cached_ref, cached_v, sem.at[1])
    fetch.start()
    per_node = cached_nodes + FRESH
    width = 128
    parent = parent_ref[...]
    none = parent.shape[0] * 128
    jump = jnp.where(parent < 0, none, parent)
    lane = lax.broadcasted_iota(jnp.int32, (groups, width), 1)
    group_row = lax.broadcasted_iota(jnp.int32, (groups, width), 0)
    path = jnp.full((groups, width), none, jnp.int32)
    for g in range(groups):
        path = jnp.where((lane == 0) & (group_row == g), child_ref[g], path)
    reach = 1
    while reach < 64:
        tables = rows_of(jump)
        ahead = jnp.where(path < none, lookup(tables, jnp.minimum(path, none - 1)), none)
        path = jnp.where((lane >= reach) & (lane < 2 * reach), pltpu.roll(ahead, reach, 1), path)
        reach *= 2
        if reach < 64:
            jump = jnp.where(jump < none, lookup(tables, jnp.minimum(jump, none - 1)), none)
    inner = path % per_node
    there = path < none
    picks = slot_sums(
        there & (path // per_node == me), inner.astype(jnp.float32), inner, cached_nodes
    )
    pick = jnp.zeros((groups, width), jnp.float32)
    for s in range(SLOTS):
        pick = jnp.where(lane == s, picks[s], pick)
    pick = pick.astype(jnp.int32)
    pick_v[...] = pick
    pick_ref[...] = pick
    copy = pltpu.make_async_copy(pick_v, pick_s, sem.at[0])
    copy.start()
    mine = jnp.sum(jnp.where(group_row == me, path, 0).astype(jnp.float32), axis=0, keepdims=True)
    mine = jnp.broadcast_to(mine, (groups, width)).astype(jnp.int32)
    there = mine < none
    lengths = lookup(rows_of(len_ref[...]), jnp.minimum(mine, none - 1)).astype(jnp.float32)
    valid = slot_sums(
        there & (mine // per_node == group_row), lengths, mine % per_node, cached_nodes
    )
    half = width // 2
    token = (lane % half).astype(jnp.float32)
    for ref, first in ((bias_a_ref, 0), (bias_b_ref, 2)):
        limit = jnp.where(lane < half, valid[first], valid[first + 1])
        ref[...] = jnp.where(token < limit, 0.0, LOW)
    copy.wait()
    fetch.wait()
    for g in range(groups):
        for s in range(2):
            node = jnp.minimum(pick_s[g, s], cached_nodes - 1)
            send_ref[g, s] = cached_v[node]


def route(parent, child_parent, node_len, cached):
    groups = child_parent.shape[0]
    _, tokens, width = cached.shape
    rows = parent.shape[0] // 128
    table = jax.ShapeDtypeStruct((groups, 128), jnp.int32)
    bias = jax.ShapeDtypeStruct((groups, 128), jnp.float32)
    out = (table, bias, bias, jax.ShapeDtypeStruct((groups, 2, tokens, width), cached.dtype))
    args = (
        parent.reshape(rows, 128),
        child_parent,
        node_len.reshape(rows, 128),
        pltpu.with_memory_space_constraint(cached, pltpu.HBM),
    )
    return pl.pallas_call(
        functools.partial(route_kernel, groups),
        out_shape=out,
        in_specs=[
            spec(args[0].shape),
            pl.BlockSpec(memory_space=pltpu.SMEM),
            spec(args[2].shape),
            pl.BlockSpec(memory_space=pl.ANY),
        ],
        out_specs=[spec(o.shape) for o in out],
        scratch_shapes=[
            pltpu.VMEM((groups, 128), jnp.int32),
            pltpu.SMEM((groups, 128), jnp.int32),
            pltpu.VMEM(cached.shape, cached.dtype),
            pltpu.SemaphoreType.DMA((2,)),
        ],
        cost_estimate=pl.CostEstimate(flops=2**24, bytes_accessed=2**21, transcendentals=0),
        name="route",
    )(*args)


def fresh_kernel(parts, pick_ref, *refs):
    hidden_refs = refs[:parts]
    weight_ref, bias_ref, cached_ref, send_ref, table, hidden = refs[parts:]
    cached_nodes, tokens, _ = cached_ref.shape
    me = lax.axis_index("tp")
    for k, ref in enumerate(hidden_refs):
        block = ref.shape[0]
        hidden[pl.ds(pl.multiple_of((me ^ k) * block, block), block), :] = ref[...]
    table[:cached_nodes] = cached_ref[...]
    total = jnp.dot(hidden[...], weight_ref[...], preferred_element_type=jnp.float32)
    rows = (total + bias_ref[...].astype(jnp.float32)[None, :]).astype(jnp.bfloat16)
    for f in range(FRESH):
        table[cached_nodes + f] = rows[f * tokens : (f + 1) * tokens]
    for g in range(send_ref.shape[0]):
        for s in range(2):
            node = jnp.clip(pick_ref[g, 2 + s], 0, cached_nodes + FRESH - 1)
            send_ref[g, s] = table[node]


def project_fresh(pick, hidden, weight, bias, cached):
    groups = pick.shape[0]
    nodes, tokens, width = cached.shape
    block, depth = hidden[0].shape
    rows = block * len(hidden)
    on_chip = pl.BlockSpec(memory_space=pltpu.VMEM)
    return pl.pallas_call(
        functools.partial(fresh_kernel, len(hidden)),
        out_shape=jax.ShapeDtypeStruct((groups, 2, tokens, width), cached.dtype),
        in_specs=[pl.BlockSpec(memory_space=pltpu.SMEM)] + [on_chip] * (len(hidden) + 3),
        out_specs=spec((groups, 2, tokens, width)),
        scratch_shapes=[
            pltpu.VMEM((nodes + FRESH, tokens, width), cached.dtype),
            pltpu.VMEM((rows, depth), cached.dtype),
        ],
        compiler_params=pltpu.CompilerParams(vmem_limit_bytes=SMALL_LIMIT),
        cost_estimate=pl.CostEstimate(
            flops=2 * rows * depth * width, bytes_accessed=8 * 2**20, transcendentals=0
        ),
        name="fresh",
    )(pick, *hidden, weight, bias, cached)


def take_keys(query, maximum, total, pieces, scale):
    rows = query.shape[0]
    head = query.shape[1]

    def score(c, piece):
        kv, adjust = piece
        s = lax.dot_general(
            query[c * ROWS : (c + 1) * ROWS, :],
            kv[:, :head],
            (((1,), (1,)), ((), ())),
            preferred_element_type=jnp.float32,
        )
        return s if adjust is None else adjust(s)

    def peak(s):
        top = s[:, :128]
        for k in range(1, s.shape[1] // 128):
            top = jnp.maximum(top, s[:, k * 128 : (k + 1) * 128])
        return top

    chunks = rows // ROWS
    now = [score(0, piece) for piece in pieces]
    for c in range(chunks):
        at = slice(c * ROWS, (c + 1) * ROWS)
        top = peak(now[0])
        for s in now[1:]:
            top = jnp.maximum(top, peak(s))
        old = maximum[at, :]
        new = jnp.maximum(old, jnp.max(top, axis=1, keepdims=True) * scale)
        maximum[at, :] = new
        factor = jnp.exp2(old - new)
        acc = total[at, :] * jnp.concatenate([factor, factor], axis=1)
        later = []
        for piece, s in zip(pieces, now):
            if c + 1 < chunks:
                later.append(score(c + 1, piece))
            weights = jnp.exp2(s * scale - new[:, :1]).astype(jnp.bfloat16)
            kv = piece[0]
            values = jnp.concatenate(
                [kv[:, head:], jnp.ones((kv.shape[0], head), jnp.bfloat16)], axis=1
            )
            acc = acc + jnp.dot(weights, values, preferred_element_type=jnp.float32)
        total[at, :] = acc
        now = later


def plain_pieces(ref):
    return [(ref.at[pl.ds(k, SUB), :], None) for k in range(0, ref.shape[0], SUB)]


def masked_pieces(ref, bias_ref):
    def adjust(k, s):
        bias = [bias_ref[row : row + 1, :] for row in range(k // 128, (k + SUB) // 128)]
        return s + jnp.concatenate(bias, axis=1)

    return [
        (ref.at[pl.ds(k, SUB), :], functools.partial(adjust, k))
        for k in range(0, ref.shape[0], SUB)
    ]


def own_piece(ref, steps):
    count = ref.shape[0]

    def adjust(s):
        row = lax.broadcasted_iota(jnp.int32, s.shape, 0) % count
        key = lax.broadcasted_iota(jnp.int32, s.shape, 1)
        seen = (row // steps == key // steps) & (key <= row)
        return jnp.where(seen, s, LOW)

    return [(ref.at[pl.ds(0, count), :], adjust)]


def load_query(q_ref, query):
    rows, head = q_ref.shape[0], query.shape[1]
    for j in range(q_ref.shape[1] // head):
        query[j * rows : (j + 1) * rows, :] = q_ref[:, j * head : (j + 1) * head]


def put_state(maximum, total, stat_ref, acc_ref):
    head = acc_ref.shape[1]
    lane = lax.broadcasted_iota(jnp.int32, stat_ref.shape, 1)
    stat_ref[...] = jnp.where(lane < head // 2, maximum[...], total[:, head:])
    acc_ref[...] = total[:, :head]


def merge_state(stat_ref, acc_ref, maximum, total):
    rows, head = acc_ref.shape
    old = jnp.broadcast_to(stat_ref[:, :1], (rows, head))
    summed = jnp.broadcast_to(stat_ref[:, head - 1 :], (rows, head))
    new = jnp.maximum(old, maximum[...])
    theirs, ours = jnp.exp2(old - new), jnp.exp2(maximum[...] - new)
    maximum[...] = new
    total[:, :head] = total[:, :head] * ours + acc_ref[...] * theirs
    total[:, head:] = total[:, head:] * ours + summed * theirs


def empty_state(maximum, total):
    maximum[...] = jnp.full_like(maximum, LOW)
    total[...] = jnp.zeros_like(total)


def first_kernel(scale, q_ref, *refs):
    prefix_refs, (stat_ref, acc_ref, query, maximum, total) = refs[:FIRST_PARTS], refs[FIRST_PARTS:]
    load_query(q_ref, query)
    empty_state(maximum, total)
    pieces = [piece for ref in prefix_refs for piece in plain_pieces(ref)]
    take_keys(query, maximum, total, pieces, scale)
    put_state(maximum, total, stat_ref, acc_ref)


def middle_kernel(scale, steps, blocks, q_ref, prefix_ref, path_ref, bias_ref, own_ref, stat_in, acc_in, maximum, total, query, stat_v, acc_v, path_v, sem):
    step = pl.program_id(0)
    pairs = ((path_ref, path_v), (stat_in, stat_v), (acc_in, acc_v))
    copies = [pltpu.make_async_copy(a, b, sem.at[k]) for k, (a, b) in enumerate(pairs)]

    @pl.when(step == 0)
    def _():
        for copy in copies:
            copy.start()
        load_query(q_ref, query)
        empty_state(maximum, total)

    @pl.when(step < blocks)
    def _():
        take_keys(query, maximum, total, plain_pieces(prefix_ref), scale)

    @pl.when(step == blocks)
    def _():
        for copy in copies:
            copy.wait()
        pieces = masked_pieces(path_v, bias_ref) + own_piece(own_ref, steps)
        take_keys(query, maximum, total, pieces, scale)
        merge_state(stat_v, acc_v, maximum, total)


def last_kernel(scale, q_ref, path_ref, bias_ref, max_in, total_in, out_ref, query, maximum, total):
    load_query(q_ref, query)
    maximum[...] = max_in[...]
    total[...] = total_in[...]
    take_keys(query, maximum, total, masked_pieces(path_ref, bias_ref), scale)
    rows, head = q_ref.shape[0], query.shape[1]
    for j in range(q_ref.shape[1] // head):
        at = slice(j * rows, (j + 1) * rows)
        out_ref[:, j * head : (j + 1) * head] = (total[at, :head] / total[at, head:]).astype(
            out_ref.dtype
        )


def attention_cost(rows, head, keys):
    return pl.CostEstimate(
        flops=8 * rows * head * keys,
        bytes_accessed=4 * keys * head,
        transcendentals=rows * keys,
    )


def per_device(
    prefix_kv,
    cached_node_states,
    fresh_hidden,
    key_value_weight,
    key_value_bias,
    decode_q,
    decoded_key_value,
    parent,
    child_parent,
    node_len,
):
    steps = 4
    head = prefix_kv.shape[2] // 2
    scale = head ** (-0.5) * LOG2E
    prefix, cached, own = prefix_kv[0], cached_node_states[0], decoded_key_value[0]
    rows = decode_q.shape[0]
    queries = rows * (decode_q.shape[1] // head)
    tp = lax.axis_size("tp")

    def moved(block, distance):
        return lax.ppermute(block, "tp", [(t, t ^ distance) for t in range(tp)])

    hidden = [fresh_hidden] * tp
    for k in (1, 2, 6, 5):
        hidden[k] = moved(fresh_hidden, k)
    hidden[7] = moved(hidden[1], 6)
    hidden[4] = moved(hidden[6], 2)
    hidden[3] = moved(hidden[1], 2)
    pick, bias_a, bias_b, send_a = route(parent, child_parent, node_len, cached)
    path_a = lax.all_to_all(send_a, "group", 0, 0, tiled=True).reshape(-1, 2 * head)

    state = (jax.ShapeDtypeStruct((queries, head), jnp.float32),) * 2
    params = pltpu.CompilerParams(vmem_limit_bytes=VMEM_LIMIT)
    scratch = [
        pltpu.VMEM((queries, head), jnp.bfloat16),
        pltpu.VMEM((queries, head), jnp.float32),
        pltpu.VMEM((queries, 2 * head), jnp.float32),
    ]
    prefix = pltpu.with_memory_space_constraint(prefix, pltpu.HBM)
    first_part = prefix.shape[0] // PART - FIRST_PARTS
    block = first_part * PART // MIDDLE_STEPS
    anywhere = pl.BlockSpec(memory_space=pl.ANY)
    state_scratch = [pltpu.VMEM(s.shape, s.dtype) for s in state]
    stat, acc = pl.pallas_call(
        functools.partial(first_kernel, scale),
        grid=(1,),
        out_shape=state,
        in_specs=[spec(decode_q.shape)]
        + [
            pl.BlockSpec((PART, 2 * head), lambda i, part=first_part + k: (part, 0))
            for k in range(FIRST_PARTS)
        ],
        out_specs=[spec(s.shape) for s in state],
        scratch_shapes=scratch,
        compiler_params=params,
        cost_estimate=attention_cost(queries, head, FIRST_PARTS * PART),
        name="attend_first",
    )(decode_q, *[prefix] * FIRST_PARTS)

    send_b = project_fresh(pick, hidden, key_value_weight, key_value_bias, cached)
    path_b = lax.all_to_all(send_b, "group", 0, 0, tiled=True).reshape(-1, 2 * head)
    path_a = pltpu.with_memory_space_constraint(path_a, pltpu.HBM)
    path_b = pltpu.with_memory_space_constraint(path_b, pltpu.VMEM)
    stat, acc = (pltpu.with_memory_space_constraint(a, pltpu.HBM) for a in (stat, acc))

    on_chip = pl.BlockSpec(memory_space=pltpu.VMEM)
    kept = (pltpu.VMEM((queries, head), jnp.float32), pltpu.VMEM((queries, 2 * head), jnp.float32))
    maximum, total = pl.pallas_call(
        functools.partial(middle_kernel, scale, steps, MIDDLE_STEPS),
        grid=(MIDDLE_STEPS + 1,),
        out_shape=kept,
        in_specs=[
            spec(decode_q.shape),
            pl.BlockSpec((block, 2 * head), lambda i: (jnp.minimum(i, MIDDLE_STEPS - 1), 0)),
            anywhere,
            spec(bias_a.shape),
            spec(own.shape),
            anywhere,
            anywhere,
        ],
        out_specs=[on_chip, on_chip],
        scratch_shapes=scratch[:1]
        + state_scratch
        + [pltpu.VMEM(path_a.shape, path_a.dtype), pltpu.SemaphoreType.DMA((3,))],
        compiler_params=params,
        cost_estimate=attention_cost(queries, head, MIDDLE_STEPS * block + path_a.shape[0]),
        name="attend_middle",
    )(decode_q, prefix, path_a, bias_a, own, stat, acc)
    maximum, total = (pltpu.with_memory_space_constraint(a, pltpu.VMEM) for a in (maximum, total))

    return pl.pallas_call(
        functools.partial(last_kernel, scale),
        out_shape=jax.ShapeDtypeStruct(decode_q.shape, jnp.bfloat16),
        in_specs=[spec(decode_q.shape), on_chip, spec(bias_b.shape), on_chip, on_chip],
        out_specs=spec(decode_q.shape),
        scratch_shapes=scratch,
        compiler_params=params,
        cost_estimate=attention_cost(queries, head, path_b.shape[0]),
        name="attend_last",
    )(decode_q, path_b, bias_b, maximum, total)


def solution(mesh):
    placed = (
        P("tp", None, None),
        P("tp", "group", None, None),
        P(("group", "tp"), None),
        P(None, "tp"),
        P("tp"),
        P("group", "tp"),
        P("tp", "group", None),
        P(),
        P(),
        P(),
    )

    return jax.shard_map(
        per_device, mesh=mesh, in_specs=placed, out_specs=P("group", "tp"), check_vma=False
    )
```

```python
import functools

import jax
import jax.numpy as jnp
from jax import lax
from jax.experimental import pallas as pl
from jax.experimental.pallas import tpu as pltpu
from jax.sharding import PartitionSpec as P

SLOTS = 4
FRESH = 2
SUB = 512
ROWS = 256
PART = 2048
FIRST_PARTS = 3
MIDDLE_STEPS = 2
LOW = -1e30
LOG2E = 1.4426950408889634
VMEM_LIMIT = 56 * 2**20
SMALL_LIMIT = 16 * 2**20


def spec(shape):
    return pl.BlockSpec(shape, lambda *_: (0,) * len(shape))


def lookup(parts, positions):
    low, high = positions & 127, positions >> 7
    result = jnp.zeros_like(positions)
    for row, part in enumerate(parts):
        table = jnp.broadcast_to(part, positions.shape)
        result = jnp.where(high == row, jnp.take_along_axis(table, low, axis=1), result)
    return result


def rows_of(table):
    return [table[row : row + 1, :] for row in range(table.shape[0])]


def ranks(flags):
    width = flags.shape[1]
    before = lax.broadcasted_iota(jnp.int32, (width, width), 0) < lax.broadcasted_iota(
        jnp.int32, (width, width), 1
    )
    return jnp.dot(
        flags.astype(jnp.bfloat16), before.astype(jnp.bfloat16), preferred_element_type=jnp.float32
    )


def slot_sums(held, values, inner, cached_nodes):
    cached = held & (inner < cached_nodes)
    fresh = held & (inner >= cached_nodes)
    rank_cached = ranks(jnp.where(cached, 1.0, 0.0))
    rank_fresh = (SLOTS - 1) - ranks(jnp.where(fresh, 1.0, 0.0))
    slot = jnp.where(cached, rank_cached, rank_fresh)
    return [
        jnp.sum(jnp.where(held & (slot == float(s)), values, 0.0), axis=1, keepdims=True)
        for s in range(SLOTS)
    ]


def route_kernel(groups, parent_ref, child_ref, len_ref, cached_ref, pick_ref, bias_a_ref, bias_b_ref, send_ref, pick_v, pick_s, cached_v, sem):
    me = lax.axis_index("group")
    cached_nodes = cached_ref.shape[0]
    fetch = pltpu.make_async_copy(cached_ref, cached_v, sem.at[1])
    fetch.start()
    per_node = cached_nodes + FRESH
    width = 128
    parent = parent_ref[...]
    none = parent.shape[0] * 128
    jump = jnp.where(parent < 0, none, parent)
    lane = lax.broadcasted_iota(jnp.int32, (groups, width), 1)
    group_row = lax.broadcasted_iota(jnp.int32, (groups, width), 0)
    path = jnp.full((groups, width), none, jnp.int32)
    for g in range(groups):
        path = jnp.where((lane == 0) & (group_row == g), child_ref[g], path)
    reach = 1
    while reach < 64:
        tables = rows_of(jump)
        ahead = jnp.where(path < none, lookup(tables, jnp.minimum(path, none - 1)), none)
        path = jnp.where((lane >= reach) & (lane < 2 * reach), pltpu.roll(ahead, reach, 1), path)
        reach *= 2
        if reach < 64:
            jump = jnp.where(jump < none, lookup(tables, jnp.minimum(jump, none - 1)), none)
    inner = path % per_node
    there = path < none
    picks = slot_sums(
        there & (path // per_node == me), inner.astype(jnp.float32), inner, cached_nodes
    )
    pick = jnp.zeros((groups, width), jnp.float32)
    for s in range(SLOTS):
        pick = jnp.where(lane == s, picks[s], pick)
    pick = pick.astype(jnp.int32)
    pick_v[...] = pick
    pick_ref[...] = pick
    copy = pltpu.make_async_copy(pick_v, pick_s, sem.at[0])
    copy.start()
    mine = jnp.sum(jnp.where(group_row == me, path, 0).astype(jnp.float32), axis=0, keepdims=True)
    mine = jnp.broadcast_to(mine, (groups, width)).astype(jnp.int32)
    there = mine < none
    lengths = lookup(rows_of(len_ref[...]), jnp.minimum(mine, none - 1)).astype(jnp.float32)
    valid = slot_sums(
        there & (mine // per_node == group_row), lengths, mine % per_node, cached_nodes
    )
    half = width // 2
    token = (lane % half).astype(jnp.float32)
    for ref, first in ((bias_a_ref, 0), (bias_b_ref, 2)):
        limit = jnp.where(lane < half, valid[first], valid[first + 1])
        ref[...] = jnp.where(token < limit, 0.0, LOW)
    copy.wait()
    fetch.wait()
    for g in range(groups):
        for s in range(2):
            node = jnp.minimum(pick_s[g, s], cached_nodes - 1)
            send_ref[g, s] = cached_v[node]


def route(parent, child_parent, node_len, cached):
    groups = child_parent.shape[0]
    _, tokens, width = cached.shape
    rows = parent.shape[0] // 128
    table = jax.ShapeDtypeStruct((groups, 128), jnp.int32)
    bias = jax.ShapeDtypeStruct((groups, 128), jnp.float32)
    out = (table, bias, bias, jax.ShapeDtypeStruct((groups, 2, tokens, width), cached.dtype))
    args = (
        parent.reshape(rows, 128),
        child_parent,
        node_len.reshape(rows, 128),
        pltpu.with_memory_space_constraint(cached, pltpu.HBM),
    )
    return pl.pallas_call(
        functools.partial(route_kernel, groups),
        out_shape=out,
        in_specs=[
            spec(args[0].shape),
            pl.BlockSpec(memory_space=pltpu.SMEM),
            spec(args[2].shape),
            pl.BlockSpec(memory_space=pl.ANY),
        ],
        out_specs=[spec(o.shape) for o in out],
        scratch_shapes=[
            pltpu.VMEM((groups, 128), jnp.int32),
            pltpu.SMEM((groups, 128), jnp.int32),
            pltpu.VMEM(cached.shape, cached.dtype),
            pltpu.SemaphoreType.DMA((2,)),
        ],
        cost_estimate=pl.CostEstimate(flops=2**24, bytes_accessed=2**21, transcendentals=0),
        name="route",
    )(*args)


def fresh_kernel(parts, pick_ref, *refs):
    hidden_refs = refs[:parts]
    weight_ref, bias_ref, cached_ref, send_ref, table, hidden = refs[parts:]
    cached_nodes, tokens, _ = cached_ref.shape
    me = lax.axis_index("tp")
    for k, ref in enumerate(hidden_refs):
        block = ref.shape[0]
        hidden[pl.ds(pl.multiple_of((me ^ k) * block, block), block), :] = ref[...]
    table[:cached_nodes] = cached_ref[...]
    total = jnp.dot(hidden[...], weight_ref[...], preferred_element_type=jnp.float32)
    rows = (total + bias_ref[...].astype(jnp.float32)[None, :]).astype(jnp.bfloat16)
    for f in range(FRESH):
        table[cached_nodes + f] = rows[f * tokens : (f + 1) * tokens]
    for g in range(send_ref.shape[0]):
        for s in range(2):
            node = jnp.clip(pick_ref[g, 2 + s], 0, cached_nodes + FRESH - 1)
            send_ref[g, s] = table[node]


def project_fresh(pick, hidden, weight, bias, cached):
    groups = pick.shape[0]
    nodes, tokens, width = cached.shape
    block, depth = hidden[0].shape
    rows = block * len(hidden)
    on_chip = pl.BlockSpec(memory_space=pltpu.VMEM)
    return pl.pallas_call(
        functools.partial(fresh_kernel, len(hidden)),
        out_shape=jax.ShapeDtypeStruct((groups, 2, tokens, width), cached.dtype),
        in_specs=[pl.BlockSpec(memory_space=pltpu.SMEM)] + [on_chip] * (len(hidden) + 3),
        out_specs=spec((groups, 2, tokens, width)),
        scratch_shapes=[
            pltpu.VMEM((nodes + FRESH, tokens, width), cached.dtype),
            pltpu.VMEM((rows, depth), cached.dtype),
        ],
        compiler_params=pltpu.CompilerParams(vmem_limit_bytes=SMALL_LIMIT),
        cost_estimate=pl.CostEstimate(
            flops=2 * rows * depth * width, bytes_accessed=8 * 2**20, transcendentals=0
        ),
        name="fresh",
    )(pick, *hidden, weight, bias, cached)


def take_keys(query, maximum, total, pieces, scale):
    rows = query.shape[0]
    head = query.shape[1]

    def score(c, piece):
        kv, adjust = piece
        s = lax.dot_general(
            query[c * ROWS : (c + 1) * ROWS, :],
            kv[:, :head],
            (((1,), (1,)), ((), ())),
            preferred_element_type=jnp.float32,
        )
        return s if adjust is None else adjust(s)

    def peak(s):
        top = s[:, :128]
        for k in range(1, s.shape[1] // 128):
            top = jnp.maximum(top, s[:, k * 128 : (k + 1) * 128])
        return top

    chunks = rows // ROWS
    now = [score(0, piece) for piece in pieces]
    for c in range(chunks):
        at = slice(c * ROWS, (c + 1) * ROWS)
        top = peak(now[0])
        for s in now[1:]:
            top = jnp.maximum(top, peak(s))
        old = maximum[at, :]
        new = jnp.maximum(old, jnp.max(top, axis=1, keepdims=True) * scale)
        maximum[at, :] = new
        factor = jnp.exp2(old - new)
        acc = total[at, :] * jnp.concatenate([factor, factor], axis=1)
        later = []
        for piece, s in zip(pieces, now):
            if c + 1 < chunks:
                later.append(score(c + 1, piece))
            weights = jnp.exp2(s * scale - new[:, :1]).astype(jnp.bfloat16)
            kv = piece[0]
            values = jnp.concatenate(
                [kv[:, head:], jnp.ones((kv.shape[0], head), jnp.bfloat16)], axis=1
            )
            acc = acc + jnp.dot(weights, values, preferred_element_type=jnp.float32)
        total[at, :] = acc
        now = later


def plain_pieces(ref):
    return [(ref.at[pl.ds(k, SUB), :], None) for k in range(0, ref.shape[0], SUB)]


def masked_pieces(ref, bias_ref):
    def adjust(k, s):
        bias = [bias_ref[row : row + 1, :] for row in range(k // 128, (k + SUB) // 128)]
        return s + jnp.concatenate(bias, axis=1)

    return [
        (ref.at[pl.ds(k, SUB), :], functools.partial(adjust, k))
        for k in range(0, ref.shape[0], SUB)
    ]


def own_piece(ref, steps):
    count = ref.shape[0]

    def adjust(s):
        row = lax.broadcasted_iota(jnp.int32, s.shape, 0) % count
        key = lax.broadcasted_iota(jnp.int32, s.shape, 1)
        seen = (row // steps == key // steps) & (key <= row)
        return jnp.where(seen, s, LOW)

    return [(ref.at[pl.ds(0, count), :], adjust)]


def load_query(q_ref, query):
    rows, head = q_ref.shape[0], query.shape[1]
    for j in range(q_ref.shape[1] // head):
        query[j * rows : (j + 1) * rows, :] = q_ref[:, j * head : (j + 1) * head]


def put_state(maximum, total, stat_ref, acc_ref):
    head = acc_ref.shape[1]
    lane = lax.broadcasted_iota(jnp.int32, stat_ref.shape, 1)
    stat_ref[...] = jnp.where(lane < head // 2, maximum[...], total[:, head:])
    acc_ref[...] = total[:, :head]


def merge_state(stat_ref, acc_ref, maximum, total):
    rows, head = acc_ref.shape
    old = jnp.broadcast_to(stat_ref[:, :1], (rows, head))
    summed = jnp.broadcast_to(stat_ref[:, head - 1 :], (rows, head))
    new = jnp.maximum(old, maximum[...])
    theirs, ours = jnp.exp2(old - new), jnp.exp2(maximum[...] - new)
    maximum[...] = new
    total[:, :head] = total[:, :head] * ours + acc_ref[...] * theirs
    total[:, head:] = total[:, head:] * ours + summed * theirs


def empty_state(maximum, total):
    maximum[...] = jnp.full_like(maximum, LOW)
    total[...] = jnp.zeros_like(total)


def first_kernel(scale, q_ref, *refs):
    prefix_refs = refs[:FIRST_PARTS]
    weight_ref, stat_ref, acc_ref, weight_v, query, maximum, total, sem = refs[FIRST_PARTS:]
    fetch = pltpu.make_async_copy(weight_ref, weight_v, sem)
    fetch.start()
    load_query(q_ref, query)
    empty_state(maximum, total)
    pieces = [piece for ref in prefix_refs for piece in plain_pieces(ref)]
    take_keys(query, maximum, total, pieces, scale)
    put_state(maximum, total, stat_ref, acc_ref)
    fetch.wait()


def middle_kernel(scale, steps, blocks, q_ref, prefix_ref, path_ref, bias_ref, own_ref, stat_in, acc_in, maximum, total, query, stat_v, acc_v, path_v, sem):
    step = pl.program_id(0)
    pairs = ((path_ref, path_v), (stat_in, stat_v), (acc_in, acc_v))
    copies = [pltpu.make_async_copy(a, b, sem.at[k]) for k, (a, b) in enumerate(pairs)]

    @pl.when(step == 0)
    def _():
        for copy in copies:
            copy.start()
        load_query(q_ref, query)
        empty_state(maximum, total)

    @pl.when(step < blocks)
    def _():
        take_keys(query, maximum, total, plain_pieces(prefix_ref), scale)

    @pl.when(step == blocks)
    def _():
        for copy in copies:
            copy.wait()
        pieces = masked_pieces(path_v, bias_ref) + own_piece(own_ref, steps)
        take_keys(query, maximum, total, pieces, scale)
        merge_state(stat_v, acc_v, maximum, total)


def last_kernel(scale, q_ref, path_ref, bias_ref, max_in, total_in, out_ref, query, maximum, total):
    load_query(q_ref, query)
    maximum[...] = max_in[...]
    total[...] = total_in[...]
    take_keys(query, maximum, total, masked_pieces(path_ref, bias_ref), scale)
    rows, head = q_ref.shape[0], query.shape[1]
    for j in range(q_ref.shape[1] // head):
        at = slice(j * rows, (j + 1) * rows)
        out_ref[:, j * head : (j + 1) * head] = (total[at, :head] / total[at, head:]).astype(
            out_ref.dtype
        )


def attention_cost(rows, head, keys):
    return pl.CostEstimate(
        flops=8 * rows * head * keys,
        bytes_accessed=4 * keys * head,
        transcendentals=rows * keys,
    )


def per_device(
    prefix_kv,
    cached_node_states,
    fresh_hidden,
    key_value_weight,
    key_value_bias,
    decode_q,
    decoded_key_value,
    parent,
    child_parent,
    node_len,
):
    steps = 4
    head = prefix_kv.shape[2] // 2
    scale = head ** (-0.5) * LOG2E
    prefix, cached, own = prefix_kv[0], cached_node_states[0], decoded_key_value[0]
    rows = decode_q.shape[0]
    queries = rows * (decode_q.shape[1] // head)
    tp = lax.axis_size("tp")

    def moved(block, distance):
        return lax.ppermute(block, "tp", [(t, t ^ distance) for t in range(tp)])

    hidden = [fresh_hidden] * tp
    for k in (1, 2, 6, 5):
        hidden[k] = moved(fresh_hidden, k)
    hidden[7] = moved(hidden[1], 6)
    hidden[4] = moved(hidden[6], 2)
    hidden[3] = moved(hidden[1], 2)
    pick, bias_a, bias_b, send_a = route(parent, child_parent, node_len, cached)
    path_a = lax.all_to_all(send_a, "group", 0, 0, tiled=True).reshape(-1, 2 * head)

    state = (jax.ShapeDtypeStruct((queries, head), jnp.float32),) * 2
    params = pltpu.CompilerParams(vmem_limit_bytes=VMEM_LIMIT)
    scratch = [
        pltpu.VMEM((queries, head), jnp.bfloat16),
        pltpu.VMEM((queries, head), jnp.float32),
        pltpu.VMEM((queries, 2 * head), jnp.float32),
    ]
    prefix = pltpu.with_memory_space_constraint(prefix, pltpu.HBM)
    first_part = prefix.shape[0] // PART - FIRST_PARTS
    block = first_part * PART // MIDDLE_STEPS
    anywhere = pl.BlockSpec(memory_space=pl.ANY)
    state_scratch = [pltpu.VMEM(s.shape, s.dtype) for s in state]
    weight = key_value_weight
    stat, acc, weight = pl.pallas_call(
        functools.partial(first_kernel, scale),
        grid=(1,),
        out_shape=(*state, pltpu.VMEM(weight.shape, weight.dtype)),
        in_specs=[spec(decode_q.shape)]
        + [
            pl.BlockSpec((PART, 2 * head), lambda i, part=first_part + k: (part, 0))
            for k in range(FIRST_PARTS)
        ]
        + [anywhere],
        out_specs=[spec(s.shape) for s in state] + [pl.BlockSpec(memory_space=pltpu.VMEM)],
        scratch_shapes=scratch + [pltpu.SemaphoreType.DMA],
        compiler_params=params,
        cost_estimate=attention_cost(queries, head, FIRST_PARTS * PART),
        name="attend_first",
    )(decode_q, *[prefix] * FIRST_PARTS, pltpu.with_memory_space_constraint(weight, pltpu.HBM))
    weight = pltpu.with_memory_space_constraint(weight, pltpu.VMEM)

    send_b = project_fresh(pick, hidden, weight, key_value_bias, cached)
    path_b = lax.all_to_all(send_b, "group", 0, 0, tiled=True).reshape(-1, 2 * head)
    path_a = pltpu.with_memory_space_constraint(path_a, pltpu.HBM)
    path_b = pltpu.with_memory_space_constraint(path_b, pltpu.VMEM)
    stat, acc = (pltpu.with_memory_space_constraint(a, pltpu.HBM) for a in (stat, acc))

    on_chip = pl.BlockSpec(memory_space=pltpu.VMEM)
    kept = (pltpu.VMEM((queries, head), jnp.float32), pltpu.VMEM((queries, 2 * head), jnp.float32))
    maximum, total = pl.pallas_call(
        functools.partial(middle_kernel, scale, steps, MIDDLE_STEPS),
        grid=(MIDDLE_STEPS + 1,),
        out_shape=kept,
        in_specs=[
            spec(decode_q.shape),
            pl.BlockSpec((block, 2 * head), lambda i: (jnp.minimum(i, MIDDLE_STEPS - 1), 0)),
            anywhere,
            spec(bias_a.shape),
            spec(own.shape),
            anywhere,
            anywhere,
        ],
        out_specs=[on_chip, on_chip],
        scratch_shapes=scratch[:1]
        + state_scratch
        + [pltpu.VMEM(path_a.shape, path_a.dtype), pltpu.SemaphoreType.DMA((3,))],
        compiler_params=params,
        cost_estimate=attention_cost(queries, head, MIDDLE_STEPS * block + path_a.shape[0]),
        name="attend_middle",
    )(decode_q, prefix, path_a, bias_a, own, stat, acc)
    maximum, total = (pltpu.with_memory_space_constraint(a, pltpu.VMEM) for a in (maximum, total))

    return pl.pallas_call(
        functools.partial(last_kernel, scale),
        out_shape=jax.ShapeDtypeStruct(decode_q.shape, jnp.bfloat16),
        in_specs=[spec(decode_q.shape), on_chip, spec(bias_b.shape), on_chip, on_chip],
        out_specs=spec(decode_q.shape),
        scratch_shapes=scratch,
        compiler_params=params,
        cost_estimate=attention_cost(queries, head, path_b.shape[0]),
        name="attend_last",
    )(decode_q, path_b, bias_b, maximum, total)


def solution(mesh):
    placed = (
        P("tp", None, None),
        P("tp", "group", None, None),
        P(("group", "tp"), None),
        P(None, "tp"),
        P("tp"),
        P("group", "tp"),
        P("tp", "group", None),
        P(),
        P(),
        P(),
    )

    return jax.shard_map(
        per_device, mesh=mesh, in_specs=placed, out_specs=P("group", "tp"), check_vma=False
    )
```
